256 devices in a mesh: ctx: 64 (over x, z, core), tp: 4 (over y).
Axes of the slice: x: 4, y: 4, z: 8, core: 2. Of those that a mesh axis runs over, the one named last changes fastest.
Arguments:
- query_head_matrix: bfloat16 [8192, 4096], P('ctx', 'tp'), may hold values from -6 to 6
- key_head_matrix: bfloat16 [8192, 1024], P('ctx', 'tp'), may hold values from -6 to 6
- value_head_matrix: bfloat16 [8192, 1024], P('ctx', 'tp'), may hold values from -6 to 6
- ssm_input: bfloat16 [8192, 8192], P('ctx', 'tp'), may hold values from -0.59765625 to 0.59765625
- log_decay: float32 [8192, 128], P('ctx', 'tp'), may hold values from -1 to 0
- state_write: bfloat16 [8192, 128], P('ctx'), may hold values from -1.796875 to 1.796875
- state_read: bfloat16 [8192, 128], P('ctx'), may hold values from -1.796875 to 1.796875
- document_ids: int32 [8192], P('ctx'), may hold values from 0 to 63, never falling along the last dimension, each value on 1 to 256 neighbouring positions
- attention_output_gradient: bfloat16 [8192, 4096], P('ctx', 'tp'), may hold values from -6 to 6
- cot_mixer: bfloat16 [8192, 8192], P('ctx', 'tp'), may hold values from -6 to 6
Outputs:
- attention_out: bfloat16 [8192, 4096], P('ctx', 'tp')
- mixer_out: bfloat16 [8192, 8192], P('ctx', 'tp')
- grad_key: bfloat16 [8192, 1024], P('ctx', 'tp')
- grad_value: bfloat16 [8192, 1024], P('ctx', 'tp')
- grad_input: bfloat16 [8192, 8192], P('ctx', 'tp')
The draws below stay inside these ranges and needn't reach their ends.
Inputs may be any that keep to these rules, and one draw needn't show every extreme that they name: `document_ids`: never falls along the sequence; each document holds 1 to 256 tokens.
All inputs are finite; a program needn't handle non-finite values.
Results may differ from the reference program's by a relative error of at most 0.0062.
Values may be sent and summed in bfloat16 or wider, within the bound.
A program may use at most 320 MiB of HBM per device.

```python
import math
import jax
import jax.numpy as jnp
import numpy as np
from jax import lax

QUERY_HEADS = 32
KEY_VALUE_HEADS = 8
HEAD_CHANNELS = 128
MIXER_HEADS = 128
SP = 64
SN = 128
TOK_DEV = 128
SPAN = 2
PACKED_TOKENS = 8192
LONGEST_DOCUMENT = 256
DOCS = 64
N_CTX = 64


def draw_key_head_matrix(key, part):
    random_base_key = jax.random.fold_in(key, 7002)
    base_values = jnp.clip(jax.random.normal(random_base_key, (PACKED_TOKENS, KEY_VALUE_HEADS, HEAD_CHANNELS), jnp.float32), -5.5, 5.5)
    return base_values.reshape(PACKED_TOKENS, KEY_VALUE_HEADS * HEAD_CHANNELS).astype(jnp.bfloat16)


def draw_query_head_matrix(key, part):
    queries_per_group = QUERY_HEADS // KEY_VALUE_HEADS
    random_base_key = jax.random.fold_in(key, 7003)
    base_values = jnp.clip(jax.random.normal(random_base_key, (PACKED_TOKENS, KEY_VALUE_HEADS, queries_per_group, HEAD_CHANNELS), jnp.float32), -5.5, 5.5)
    return base_values.reshape(PACKED_TOKENS, QUERY_HEADS * HEAD_CHANNELS).astype(jnp.bfloat16)


def draw_log_decay(key, part):
    rate_key = jax.random.fold_in(key, 7010)
    step_key = jax.random.fold_in(key, 7011)
    spike_random_key = jax.random.fold_in(key, 7012)
    size_key = jax.random.fold_in(key, 7013)
    spread = jax.random.uniform(rate_key, (MIXER_HEADS,), jnp.float32)
    low_log = math.log(0.1 / LONGEST_DOCUMENT)
    rates = jnp.exp(low_log + spread * math.log(LONGEST_DOCUMENT / 3.0))
    step_len = jax.random.uniform(step_key, (PACKED_TOKENS, MIXER_HEADS), jnp.float32, 0.5, 1.5)
    match_flags = jax.random.uniform(spike_random_key, (PACKED_TOKENS, MIXER_HEADS), jnp.float32) < 3.0 / LONGEST_DOCUMENT
    jumps = jnp.where(match_flags, jax.random.uniform(size_key, (PACKED_TOKENS, MIXER_HEADS), jnp.float32, 0.22, 0.69), 0.0)
    return -(rates[None, :] * step_len + jumps)


def shard_levels(key, dims, shards, low, largest):
    def one(axis_at, parts):
        draws = jax.random.uniform(jax.random.fold_in(jax.random.fold_in(key, 6), axis_at), (parts,), jnp.float32, low / len(shards), largest / len(shards))
        return jnp.repeat(jnp.exp(draws), dims[axis_at] // parts).reshape((-1,) + (1,) * (len(dims) - axis_at - 1))

    factor_of = one(*shards[0])
    for cut in shards[1:]:
        factor_of = factor_of * one(*cut)
    return factor_of


def profile(count, total, most, slope):
    weights = [(1 << 20) // math.isqrt(standing ** slope) + 1 for standing in range(2, count + 1)]
    surplus, counts = total - most - (count - 1), [1] * (count - 1)
    while surplus > 0:
        free = [i for i in range(count - 1) if counts[i] < most]
        whole, left = sum([weights[i] for i in free]), surplus
        for i in free:
            addition = min(most - counts[i], max(1, left * weights[i] // whole), surplus)
            counts[i] = counts[i] + addition
            surplus = surplus - addition
    return np.array([most] + counts)


def ragged_sizes(stream_key, count, total, most, skew):
    if count == 2:
        one = jax.random.randint(stream_key, (), max(1, total - most), min(most, total - 1) + 1)
        return jnp.stack([one, total - one])
    lengths = jnp.asarray(profile(count, total, most, skew), jnp.int32)
    twos = (count - 1) // 2
    giver, receiver = lengths[1:1 + 2 * twos:2], lengths[2:2 + 2 * twos:2]
    room = jnp.minimum(giver - 1, most - receiver)
    passed = jax.random.randint(jax.random.fold_in(stream_key, 1), (twos,), 0, 1 << 20) % (room + 1)
    lengths = lengths.at[1:1 + 2 * twos:2].set(giver - passed).at[2:2 + 2 * twos:2].set(receiver + passed)
    return lengths[jax.random.permutation(jax.random.fold_in(stream_key, 2), count)]


def normal_values(key, extent, width, bound, cuts=(), held_as=jnp.bfloat16):
    result = jax.random.normal(key, extent, jnp.float32) * width
    if len(cuts) > 0:
        result = shard_levels(key, extent, cuts, -0.22, 0.18) * result
    return jnp.clip(result, min=-bound, max=bound).astype(held_as)


def setup_inputs(seed: int = 0) -> dict:
    streams_of = jax.random.split(jax.random.key(seed), 11)
    query_head_matrix = draw_query_head_matrix(jax.random.fold_in(streams_of[10], 71), 0)
    key_head_matrix = draw_key_head_matrix(jax.random.fold_in(streams_of[10], 71), 0)
    value_head_matrix = normal_values(streams_of[2], (PACKED_TOKENS, KEY_VALUE_HEADS * HEAD_CHANNELS), 1.0, 6.0, ((0, 64), (1, 4)))
    ssm_input = normal_values(streams_of[3], (PACKED_TOKENS, MIXER_HEADS * SP), 0.1, 0.59765625, ((0, 64), (1, 4)))
    log_decay = draw_log_decay(jax.random.fold_in(streams_of[10], 71), 0)
    state_write = normal_values(streams_of[5], (PACKED_TOKENS, SN), 0.3, 1.796875, ((0, 64),))
    state_read = normal_values(streams_of[6], (PACKED_TOKENS, SN), 0.3, 1.796875, ((0, 64),))
    document_ids = jnp.searchsorted(jnp.cumsum(ragged_sizes(streams_of[7], DOCS, PACKED_TOKENS, LONGEST_DOCUMENT, 2)), jnp.arange(PACKED_TOKENS), side="right").astype(jnp.int32)
    attention_output_gradient = normal_values(streams_of[8], (PACKED_TOKENS, QUERY_HEADS * HEAD_CHANNELS), 1.0, 6.0, ((0, 64), (1, 4)))
    cot_mixer = normal_values(streams_of[9], (PACKED_TOKENS, MIXER_HEADS * SP), 1.0, 6.0, ((0, 64), (1, 4)))
    return {"query_head_matrix": query_head_matrix, "key_head_matrix": key_head_matrix, "value_head_matrix": value_head_matrix, "ssm_input": ssm_input, "log_decay": log_decay, "state_write": state_write, "state_read": state_read, "document_ids": document_ids, "attention_output_gradient": attention_output_gradient, "cot_mixer": cot_mixer}


def mixer_block_pieces(decays, writes, reads, doc_row, prev_doc):
    tokens = decays.shape[0]
    running = jnp.cumsum(decays, axis=0).T
    row_ids = jnp.arange(tokens)
    inside = (row_ids[:, None] >= row_ids[None, :]) & (doc_row[:, None] == doc_row[None, :])
    log_gaps = running[:, :, None] - running[:, None, :]
    decay_mat = jnp.exp(jnp.where(inside[None], log_gaps, -jnp.inf))
    scores = jnp.dot(reads, writes.T, preferred_element_type=jnp.float32)
    weights = (decay_mat * scores[None]).astype(jnp.bfloat16)
    entry_w = jnp.exp(running) * (doc_row == prev_doc).astype(jnp.float32)[None]
    read_w = (entry_w[:, :, None] * reads.astype(jnp.float32)[None]).astype(jnp.bfloat16)
    exit_w = jnp.exp(running[:, -1:] - running) * (doc_row == doc_row[-1]).astype(jnp.float32)[None]
    write_w = (exit_w[:, :, None] * writes.astype(jnp.float32)[None]).astype(jnp.bfloat16)
    block_gain = jnp.exp(running[:, -1]) * (doc_row[-1] == prev_doc).astype(jnp.float32)
    weights, read_w, write_w = lax.optimization_barrier((weights, read_w, write_w))
    return (weights, read_w, write_w, block_gain)

def mixer_reference(ssm_input, log_decay, state_write, state_read, document_ids, cot_mixer):
    blocks = N_CTX
    input_blocks = ssm_input.reshape(blocks, TOK_DEV, MIXER_HEADS, SP)
    cot_blocks = cot_mixer.reshape(blocks, TOK_DEV, MIXER_HEADS, SP)
    decay_blocks = log_decay.reshape(blocks, TOK_DEV, MIXER_HEADS)
    write_blocks = state_write.reshape(blocks, TOK_DEV, SN)
    read_blocks = state_read.reshape(blocks, TOK_DEV, SN)
    doc_blocks = document_ids.reshape(blocks, TOK_DEV)
    prev_docs = jnp.concatenate([jnp.full((1,), -1, jnp.int32), doc_blocks[:-1, -1].astype(jnp.int32)])

    def first_pass(packed):
        inputs, cot_rows, decays, writes, reads, doc_row, prev_doc = packed
        weights, read_w, write_w, block_gain = mixer_block_pieces(decays, writes, reads, doc_row, prev_doc)
        block_state = jnp.einsum('shp,hsn->hpn', inputs.astype(jnp.float32), write_w.astype(jnp.float32))
        block_back = jnp.einsum('thp,htn->hpn', cot_rows.astype(jnp.float32), read_w.astype(jnp.float32))
        return (block_gain, block_state, block_back)
    block_gains, block_states, block_backs = lax.map(first_pass, (input_blocks, cot_blocks, decay_blocks, write_blocks, read_blocks, doc_blocks, prev_docs))

    def forward_step(running_sum, pair_in):
        return (pair_in[0][:, None, None] * running_sum + pair_in[1], running_sum)

    def backward_step(running_sum, pair_in):
        return (pair_in[1] + pair_in[0][:, None, None] * running_sum, running_sum)
    start_zero = jnp.zeros((MIXER_HEADS, SP, SN), jnp.float32)
    _, carry_in = lax.scan(forward_step, start_zero, (block_gains, block_states))
    _, carry_out = lax.scan(backward_step, start_zero, (block_gains, block_backs), reverse=True)

    def second_pass(packed):
        inputs, cot_rows, decays, writes, reads, doc_row, prev_doc, state_in, state_out = packed
        weights, read_w, write_w, block_gain = mixer_block_pieces(decays, writes, reads, doc_row, prev_doc)
        weight_f32 = weights.astype(jnp.float32)
        mixed_out = jnp.einsum('hts,shp->thp', weight_f32, inputs.astype(jnp.float32))
        mixed_out = mixed_out + jnp.einsum('hpn,htn->thp', state_in, read_w.astype(jnp.float32), precision=lax.Precision.HIGHEST)
        grad_rows = jnp.einsum('hts,thp->shp', weight_f32, cot_rows.astype(jnp.float32))
        grad_rows = grad_rows + jnp.einsum('hpn,hsn->shp', state_out, write_w.astype(jnp.float32), precision=lax.Precision.HIGHEST)
        return (mixed_out.astype(jnp.bfloat16), grad_rows.astype(jnp.bfloat16))
    mixed_all, grad_all = lax.map(second_pass, (input_blocks, cot_blocks, decay_blocks, write_blocks, read_blocks, doc_blocks, prev_docs, carry_in, carry_out))
    return (mixed_all.reshape(PACKED_TOKENS, MIXER_HEADS * SP), grad_all.reshape(PACKED_TOKENS, MIXER_HEADS * SP))

def attention_reference(query_head_matrix, key_head_matrix, value_head_matrix, document_ids, attention_output_gradient):
    queries_per_group = QUERY_HEADS // KEY_VALUE_HEADS
    inv_root = 1.0 / math.sqrt(HEAD_CHANNELS)
    leading_rows = SPAN * TOK_DEV
    attention_span = (SPAN + 1) * TOK_DEV
    query_rows_all = query_head_matrix.reshape(PACKED_TOKENS, KEY_VALUE_HEADS, queries_per_group, HEAD_CHANNELS)
    output_gradient_all = attention_output_gradient.reshape(PACKED_TOKENS, KEY_VALUE_HEADS, queries_per_group, HEAD_CHANNELS)
    padded_keys = jnp.concatenate([jnp.zeros((leading_rows, KEY_VALUE_HEADS * HEAD_CHANNELS), key_head_matrix.dtype), key_head_matrix], axis=0)
    padded_values = jnp.concatenate([jnp.zeros((leading_rows, KEY_VALUE_HEADS * HEAD_CHANNELS), value_head_matrix.dtype), value_head_matrix], axis=0)
    doc_pad = jnp.concatenate([jnp.full((leading_rows,), -1, jnp.int32), document_ids.astype(jnp.int32)])

    def attend_block(running_sums, block_no):
        key_sums, value_sums = running_sums
        starting_row = (block_no * TOK_DEV).astype(jnp.int32)
        query_block_rows = lax.dynamic_slice_in_dim(query_rows_all, starting_row, TOK_DEV, 0).astype(jnp.float32)
        output_gradient_block = lax.dynamic_slice_in_dim(output_gradient_all, starting_row, TOK_DEV, 0).astype(jnp.float32)
        key_span_rows = lax.dynamic_slice_in_dim(padded_keys, starting_row, attention_span, 0).reshape(attention_span, KEY_VALUE_HEADS, HEAD_CHANNELS).astype(jnp.float32)
        value_span_rows = lax.dynamic_slice_in_dim(padded_values, starting_row, attention_span, 0).reshape(attention_span, KEY_VALUE_HEADS, HEAD_CHANNELS).astype(jnp.float32)
        doc_win = lax.dynamic_slice_in_dim(doc_pad, starting_row, attention_span, 0)
        doc_query = lax.dynamic_slice_in_dim(document_ids.astype(jnp.int32), starting_row, TOK_DEV, 0)
        key_pos = starting_row - leading_rows + jnp.arange(attention_span, dtype=jnp.int32)
        query_pos = starting_row + jnp.arange(TOK_DEV, dtype=jnp.int32)
        inside = (doc_win[None, :] == doc_query[:, None]) & (key_pos[None, :] <= query_pos[:, None])
        scores = jnp.einsum('tgid,sgd->gits', query_block_rows, key_span_rows) * inv_root
        scores = jnp.where(inside[None, None], scores, -jnp.inf)
        row_peak = lax.optimization_barrier(jnp.max(scores, axis=-1, keepdims=True))
        raised = jnp.exp(scores - row_peak)
        prob_mat = lax.optimization_barrier((raised / lax.optimization_barrier(jnp.sum(raised, axis=-1, keepdims=True))).astype(jnp.bfloat16))
        probability_single = prob_mat.astype(jnp.float32)
        out_block = jnp.einsum('gits,sgd->tgid', probability_single, value_span_rows).astype(jnp.bfloat16)
        prob_grad = jnp.einsum('tgid,sgd->gits', output_gradient_block, value_span_rows)
        inner_sum = lax.optimization_barrier(jnp.sum(probability_single * prob_grad, axis=-1, keepdims=True))
        score_gradient = lax.optimization_barrier((probability_single * (prob_grad - inner_sum) * inv_root).astype(jnp.bfloat16))
        key_gradient = jnp.einsum('wpza,zwpo->awo', score_gradient.astype(jnp.float32), query_block_rows).reshape(attention_span, KEY_VALUE_HEADS * HEAD_CHANNELS)
        value_gradient = jnp.einsum('wpza,zwpo->awo', probability_single, output_gradient_block).reshape(attention_span, KEY_VALUE_HEADS * HEAD_CHANNELS)
        key_sums = lax.dynamic_update_slice_in_dim(key_sums, lax.dynamic_slice_in_dim(key_sums, starting_row, attention_span, 0) + key_gradient, starting_row, 0)
        value_sums = lax.dynamic_update_slice_in_dim(value_sums, lax.dynamic_slice_in_dim(value_sums, starting_row, attention_span, 0) + value_gradient, starting_row, 0)
        return ((key_sums, value_sums), out_block.reshape(TOK_DEV, QUERY_HEADS * HEAD_CHANNELS))
    initial_sums = jnp.zeros((leading_rows + PACKED_TOKENS, KEY_VALUE_HEADS * HEAD_CHANNELS), jnp.float32)
    final_sums, out_blocks = lax.scan(attend_block, (initial_sums, initial_sums), jnp.arange(N_CTX, dtype=jnp.int32))
    attention_out = out_blocks.reshape(PACKED_TOKENS, QUERY_HEADS * HEAD_CHANNELS)
    grad_key = final_sums[0][leading_rows:].astype(jnp.bfloat16)
    grad_value = final_sums[1][leading_rows:].astype(jnp.bfloat16)
    return (attention_out, grad_key, grad_value)

def reference(query_head_matrix, key_head_matrix, value_head_matrix, ssm_input, log_decay, state_write, state_read, document_ids, attention_output_gradient, cot_mixer):
    attention_out, grad_key, grad_value = attention_reference(query_head_matrix, key_head_matrix, value_head_matrix, document_ids, attention_output_gradient)
    mixer_out, grad_input = mixer_reference(ssm_input, log_decay, state_write, state_read, document_ids, cot_mixer)
    return (attention_out, mixer_out, grad_key, grad_value, grad_input)
```

```python
import math

import jax
import jax.numpy as jnp
from jax import lax
from jax.experimental import pallas as pl
from jax.experimental.pallas import tpu as pltpu
from jax.sharding import PartitionSpec as P

HEAD_CHANNELS = 128
CHUNKS = 4
MESH = pl.DeviceIdType.MESH
F32 = jnp.float32
BF16 = jnp.bfloat16


def dot(a, b, contract=((1,), (0,)), precision=None):
    return lax.dot_general(a, b, (contract, ((), ())), precision=precision, preferred_element_type=F32)


def step_kernel(
    q_in, k_in, v_in, x_in, ld_in, sw_in, sr_in, doc_in, do_in, cm_in,
    ao_out, mo_out, gk_out, gv_out, gx_out,
    qb, dob, xc, ldb, srw, srwt, docs, kw, vw, sc, lt, st, mbuf, cz, zbuf, lbuf, gain, gmate,
    local, outb, aob, pt, dst, bias, gs, gr, gown, gkb, gmask, lsem, ssem, rsem,
):
    tokens = qb.shape[0]
    groups = k_in.shape[1] // HEAD_CHANNELS
    per_group = q_in.shape[1] // k_in.shape[1]
    heads = ld_in.shape[1]
    chunk_cols = x_in.shape[1] // CHUNKS
    chunk_heads = heads // CHUNKS
    half = chunk_cols // chunk_heads
    inv_root = 1.0 / math.sqrt(HEAD_CHANNELS)

    count = lax.axis_size("ctx")
    me = lax.axis_index("ctx")
    row = lax.axis_index("tp")
    side = lax.rem(me, 2)
    other = 1 - side
    after1 = lax.rem(me + 1, count)
    after2 = lax.rem(me + 2, count)
    before1 = lax.rem(me + count - 1, count)
    before2 = lax.rem(me + count - 2, count)
    mate = me + 1 - 2 * side
    outer = lax.rem(me - 1 + 2 * side + count, count)

    local_at = [0]

    def load(src, dst_ref):
        copy = pltpu.make_async_copy(src, dst_ref, lsem.at[local_at[0]])
        local_at[0] += 1
        copy.start()
        return copy

    remote_at = [0]

    def send(src, dst_ref, target):
        n = remote_at[0]
        remote_at[0] += 1
        return pltpu.make_async_remote_copy(
            src_ref=src, dst_ref=dst_ref, send_sem=ssem.at[n], recv_sem=rsem.at[n],
            device_id=(target, row), device_id_type=MESH,
        )

    doc_load = load(doc_in, docs.at[2])
    ld_load = load(ld_in, ldb)
    sw_load = load(sw_in, srw.at[0])
    sr_load = load(sr_in, srw.at[1])
    barrier = pltpu.get_barrier_semaphore()
    for target in (after1, after2, before1, before2):
        pl.semaphore_signal(barrier, inc=1, device_id=(target, row), device_id_type=MESH)
    x_loads = []
    for c in range(CHUNKS):
        cols = pl.ds(c * chunk_cols, chunk_cols)
        x_loads.append((load(x_in.at[:, cols], xc.at[0, c]), load(cm_in.at[:, cols], xc.at[1, c])))
    k_load = load(k_in, kw.at[2])
    v_load = load(v_in, vw.at[2])
    q_load = load(q_in, qb)
    do_load = load(do_in, dob)

    rows_i = lax.broadcasted_iota(jnp.int32, (tokens, tokens), 0)
    cols_i = lax.broadcasted_iota(jnp.int32, (tokens, tokens), 1)
    tril = (rows_i >= cols_i).astype(F32)
    ld_load.wait()
    decays = ldb[...]
    lam = dot(tril, decays, precision=lax.Precision.HIGHEST)
    lam_t = dot(decays, tril, ((0,), (1,)), precision=lax.Precision.HIGHEST)
    for c in range(CHUNKS):
        lt[c] = lam_t[c * chunk_heads : (c + 1) * chunk_heads]
    doc_load.wait()

    doc_row = docs[2].astype(F32)
    doc_rows = jnp.broadcast_to(doc_row, (tokens, tokens))
    doc_cols = doc_rows.T
    doc_last = doc_row[:, tokens - 1 : tokens]

    sw_load.wait()
    sr_load.wait()
    writes = srw[0]
    reads = srw[1]
    srwt[0] = writes.T
    srwt[1] = reads.T

    pl.semaphore_wait(barrier, 4)
    doc_sends = [send(docs.at[2], docs.at[1], after1), send(docs.at[2], docs.at[0], after2)]
    for copy in doc_sends:
        copy.start()
    kv_sends = [
        send(k_in, kw.at[1], after1), send(v_in, vw.at[1], after1),
        send(k_in, kw.at[0], after2), send(v_in, vw.at[0], after2),
    ]
    for copy in kv_sends:
        copy.start()

    spread_at = lax.broadcasted_iota(jnp.int32, (2 * heads, chunk_cols), 0)
    spread_lane = lax.broadcasted_iota(jnp.int32, (2 * heads, chunk_cols), 1)

    def spread(values, slot):
        high = values.astype(BF16)
        low = (values - high.astype(F32)).astype(BF16)
        both = jnp.concatenate([high, low], axis=1)
        for c in range(CHUNKS):
            head = spread_lane // half + c * chunk_heads
            hot = ((spread_at == head) | (spread_at == head + heads)).astype(F32).astype(BF16)
            sc[slot, c] = dot(both, hot)

    lam_last = lam[tokens - 1 : tokens, :]
    doc_cols_h = doc_cols[:, :heads]
    exit_w = jnp.where(doc_cols_h == doc_last, jnp.exp(lam_last - lam), 0.0)
    spread(exit_w, 0)

    same = doc_rows == doc_cols
    score = dot(reads, writes, ((1,), (1,)))
    score_t = dot(writes, reads, ((1,), (1,)))
    gmask[0] = jnp.where(same & (rows_i >= cols_i), score, 0.0)
    gmask[1] = jnp.where(same & (cols_i >= rows_i), score_t, 0.0)

    doc_sends[0].wait_recv()
    doc1_row = jnp.where(me >= 1, docs[1].astype(F32), -1.0)
    prev = doc1_row[:, tokens - 1 : tokens]
    entry_w = jnp.where(doc_cols_h == prev, jnp.exp(lam), 0.0)
    spread(entry_w, 1)
    for c in range(CHUNKS):
        gain[c] = sc[1, c][tokens - 1 : tokens, :]

    for pair in x_loads:
        for copy in pair:
            copy.wait()
    gain_send = send(gain, gmate, mate)
    gain_send.start()

    def state(d, c):
        scaled = (xc[d, c].astype(F32) * sc[d, c]).astype(BF16)
        st[d, c] = dot(srwt[d], scaled).astype(BF16)

    mate_sends = []
    for c in range(CHUNKS):
        state(side, c)
        copy = send(st.at[side, c], mbuf.at[c], mate)
        copy.start()
        mate_sends.append(copy)
    for c in range(CHUNKS):
        state(other, c)
    outer_sends = []
    for c in range(CHUNKS):
        mate_sends[c].wait_recv()
        cz[c] = (st[other, c].astype(F32) + gain[c] * mbuf[c].astype(F32)).astype(BF16)
        copy = send(cz.at[c], zbuf.at[c], outer)
        copy.start()
        outer_sends.append(copy)

    lane = lax.broadcasted_iota(jnp.int32, (1, 2 * half), 1)
    low_half = (lane < half).astype(F32).astype(BF16)
    high_half = (lane >= half).astype(F32).astype(BF16)

    def inside_block(c, carry):
        for j in range(chunk_heads // 2):
            fwd = []
            bwd = []
            for i in range(2):
                h = 2 * j + i
                lam_rows = jnp.broadcast_to(lt[c, h : h + 1, :], (tokens, tokens))
                decay = jnp.exp(-jnp.abs(lam_rows.T - lam_rows))
                fwd.append((decay * gmask[0]).astype(BF16))
                bwd.append((decay * gmask[1]).astype(BF16))
            cols = slice(2 * j * half, (2 * j + 2) * half)
            for d, weights in ((0, fwd), (1, bwd)):
                tile = xc[d, c, :, cols]
                local[d, c, :, cols] = dot(
                    jnp.concatenate(weights, axis=1),
                    jnp.concatenate([tile * low_half, tile * high_half], axis=0),
                )
        return carry

    lax.fori_loop(0, CHUNKS, inside_block, 0)

    doc_sends[1].wait_recv()
    doc2_row = jnp.where(me >= 2, docs[0].astype(F32), -1.0)
    minus = -1e30
    bias[0:tokens] = jnp.where(jnp.broadcast_to(doc2_row, (tokens, tokens)).T == doc_rows, 0.0, minus)
    bias[tokens : 2 * tokens] = jnp.where(
        jnp.broadcast_to(doc1_row, (tokens, tokens)).T == doc_rows, 0.0, minus
    )
    bias[2 * tokens : 3 * tokens] = jnp.where(same & (cols_i >= rows_i), 0.0, minus)
    k_load.wait()
    v_load.wait()
    q_load.wait()
    do_load.wait()
    for copy in kv_sends:
        copy.wait_recv()
    grad_sends = []
    for g in range(groups):
        cols = slice(g * HEAD_CHANNELS, (g + 1) * HEAD_CHANNELS)
        keys = jnp.concatenate([kw[n, :, cols] for n in range(3)], axis=0)
        values = jnp.concatenate([vw[n, :, cols] for n in range(3)], axis=0)
        values_t = values.T
        for i in range(per_group):
            h = g * per_group + i
            hcols = slice(h * HEAD_CHANNELS, (h + 1) * HEAD_CHANNELS)
            icols = slice(i * tokens, (i + 1) * tokens)
            raw = dot(keys, qb[:, hcols], ((1,), (1,))) + bias[...]
            peak = jnp.max(raw, axis=0, keepdims=True)
            raised = jnp.exp((raw - peak) * inv_root)
            probs = (raised * (1.0 / jnp.sum(raised, axis=0, keepdims=True))).astype(BF16)
            pt[:, icols] = probs
            aob[:, hcols] = dot(values_t, probs).T.astype(BF16)
            prob_grad = dot(values, dob[:, hcols], ((1,), (1,)))
            single = probs.astype(F32)
            inner = jnp.sum(single * prob_grad, axis=0, keepdims=True)
            dst[:, icols] = (single * (prob_grad - inner) * inv_root).astype(BF16)
        q_rows = jnp.concatenate(
            [qb[:, h * HEAD_CHANNELS : (h + 1) * HEAD_CHANNELS] for h in range(g * per_group, (g + 1) * per_group)], axis=0
        )
        do_rows = jnp.concatenate(
            [dob[:, h * HEAD_CHANNELS : (h + 1) * HEAD_CHANNELS] for h in range(g * per_group, (g + 1) * per_group)], axis=0
        )
        for n, grad in enumerate((dot(dst[...], q_rows), dot(pt[...], do_rows))):
            gs[g, 0, n] = grad[0:tokens].astype(BF16)
            gs[g, 1, n] = grad[tokens : 2 * tokens].astype(BF16)
            gown[n, :, cols] = grad[2 * tokens :]
        for slot, target in ((1, before1), (0, before2)):
            copy = send(gs.at[g, slot], gr.at[g, slot], target)
            copy.start()
            grad_sends.append(copy)
    ao_store = load(aob, ao_out)

    relay_sends = []
    for c in range(CHUNKS):
        outer_sends[c].wait_recv()
        copy = send(zbuf.at[c], lbuf.at[c], mate)
        copy.start()
        relay_sends.append(copy)

    def finish(d, c, carried):
        outb[d, c] = (local[d, c] + sc[1 - d, c] * dot(srw[1 - d], carried)).astype(BF16)

    for c in range(CHUNKS):
        finish(side, c, zbuf[c])
    gain_send.wait_recv()
    for c in range(CHUNKS):
        relay_sends[c].wait_recv()
        finish(other, c, (mbuf[c].astype(F32) + gmate[c] * lbuf[c].astype(F32)).astype(BF16))
    stores = [ao_store]
    for c in range(CHUNKS):
        cols = pl.ds(c * chunk_cols, chunk_cols)
        stores.append(load(outb.at[0, c], mo_out.at[:, cols]))
        stores.append(load(outb.at[1, c], gx_out.at[:, cols]))

    for copy in grad_sends:
        copy.wait_recv()
    for n in range(2):
        for g in range(groups):
            cols = slice(g * HEAD_CHANNELS, (g + 1) * HEAD_CHANNELS)
            total = gown[n, :, cols] + gr[g, 1, n].astype(F32) + gr[g, 0, n].astype(F32)
            gkb[n, :, cols] = total.astype(BF16)
    stores.append(load(gkb.at[0], gk_out))
    stores.append(load(gkb.at[1], gv_out))

    for copy in doc_sends + kv_sends + [gain_send] + mate_sends + outer_sends + grad_sends + relay_sends:
        copy.wait_send()
    for copy in stores:
        copy.wait()


def shards(q, k, v, x, ld, sw, sr, doc, do, cm):
    tokens = q.shape[0]
    groups = k.shape[1] // HEAD_CHANNELS
    per_group = q.shape[1] // k.shape[1]
    heads = ld.shape[1]
    states = sw.shape[1]
    chunk_cols = x.shape[1] // CHUNKS
    span = 3 * tokens
    remotes = 6 + 1 + 3 * CHUNKS + 2 * groups
    locals_ = 4 + 2 * CHUNKS + 4 + 1 + 2 * CHUNKS + 2
    vmem = pltpu.VMEM
    anywhere = pl.BlockSpec(memory_space=pl.ANY)
    shape = jax.ShapeDtypeStruct
    return pl.pallas_call(
        step_kernel,
        out_shape=(
            shape(q.shape, BF16), shape(x.shape, BF16), shape(k.shape, BF16), shape(v.shape, BF16), shape(x.shape, BF16),
        ),
        in_specs=[anywhere] * 10,
        out_specs=[anywhere] * 5,
        scratch_shapes=[
            vmem(q.shape, BF16),
            vmem(q.shape, BF16),
            vmem((2, CHUNKS, tokens, chunk_cols), BF16),
            vmem(ld.shape, F32),
            vmem((2, tokens, states), BF16),
            vmem((2, states, tokens), BF16),
            vmem((3, 1, tokens), jnp.int32),
            vmem((3,) + k.shape, BF16),
            vmem((3,) + v.shape, BF16),
            vmem((2, CHUNKS, tokens, chunk_cols), F32),
            vmem((CHUNKS, heads // CHUNKS, tokens), F32),
            vmem((2, CHUNKS, states, chunk_cols), BF16),
            vmem((CHUNKS, states, chunk_cols), BF16),
            vmem((CHUNKS, states, chunk_cols), BF16),
            vmem((CHUNKS, states, chunk_cols), BF16),
            vmem((CHUNKS, states, chunk_cols), BF16),
            vmem((CHUNKS, 1, chunk_cols), F32),
            vmem((CHUNKS, 1, chunk_cols), F32),
            vmem((2, CHUNKS, tokens, chunk_cols), F32),
            vmem((2, CHUNKS, tokens, chunk_cols), BF16),
            vmem(q.shape, BF16),
            vmem((span, per_group * tokens), BF16),
            vmem((span, per_group * tokens), BF16),
            vmem((span, tokens), F32),
            vmem((groups, 2, 2, tokens, HEAD_CHANNELS), BF16),
            vmem((groups, 2, 2, tokens, HEAD_CHANNELS), BF16),
            vmem((2,) + k.shape, F32),
            vmem((2,) + k.shape, BF16),
            vmem((2, tokens, tokens), F32),
            pltpu.SemaphoreType.DMA((locals_,)),
            pltpu.SemaphoreType.DMA((remotes,)),
            pltpu.SemaphoreType.DMA((remotes,)),
        ],
        compiler_params=pltpu.CompilerParams(collective_id=0, has_side_effects=True, vmem_limit_bytes=48 << 20),
        name="step",
    )(q, k, v, x, ld, sw, sr, doc.reshape(1, tokens), do, cm)


def solution(mesh):
    both = P("ctx", "tp")
    return jax.shard_map(
        shards,
        mesh=mesh,
        in_specs=(both, both, both, both, both, P("ctx", None), P("ctx", None), P("ctx"), both, both),
        out_specs=(both,) * 5,
        check_vma=False,
    )
```

```python
import math

import jax
import jax.numpy as jnp
from jax import lax
from jax.experimental import pallas as pl
from jax.experimental.pallas import tpu as pltpu
from jax.sharding import PartitionSpec as P

HEAD_CHANNELS = 128
CHUNKS = 4
MESH = pl.DeviceIdType.MESH
F32 = jnp.float32
BF16 = jnp.bfloat16


def dot(a, b, contract=((1,), (0,)), precision=None):
    return lax.dot_general(a, b, (contract, ((), ())), precision=precision, preferred_element_type=F32)


def step_kernel(
    q_in, k_in, v_in, x_in, ld_in, sw_in, sr_in, doc_in, do_in, cm_in,
    ao, mix, gkv,
    qb, dob, xc, ldb, srw, srwt, docs, kvw, sc, lt, st, mbuf, cz, zbuf, lbuf, gain, gmate,
    local, pt, dst, bias, gs, gr, gown, gmask, lsem, ssem, rsem,
):
    tokens = qb.shape[0]
    groups = k_in.shape[1] // HEAD_CHANNELS
    per_group = q_in.shape[1] // k_in.shape[1]
    heads = ld_in.shape[0]
    chunk_cols = x_in.shape[1] // CHUNKS
    chunk_heads = heads // CHUNKS
    half = chunk_cols // chunk_heads
    inv_root = 1.0 / math.sqrt(HEAD_CHANNELS)
    square = (tokens, tokens)

    count = lax.axis_size("ctx")
    me = lax.axis_index("ctx")
    row = lax.axis_index("tp")
    side = lax.rem(me, 2)
    other = 1 - side
    mate = me + 1 - 2 * side
    outer = me - 1 + 2 * side
    has_before1 = me >= 1
    has_before2 = me >= 2
    has_after1 = me < count - 1
    has_after2 = me < count - 2
    has_outer = has_before1 & has_after1
    is_first = side == 0

    local_at = [0]

    def load(src, dst_ref):
        copy = pltpu.make_async_copy(src, dst_ref, lsem.at[local_at[0]])
        local_at[0] += 1
        copy.start()
        return copy

    remote_at = [0]

    def send(src, dst_ref, target):
        n = remote_at[0]
        remote_at[0] += 1
        return pltpu.make_async_remote_copy(
            src_ref=src, dst_ref=dst_ref, send_sem=ssem.at[n], recv_sem=rsem.at[n],
            device_id=(target, row), device_id_type=MESH,
        )

    docs_mate = send(docs.at[2], docs.at[1 + 2 * side], mate)
    docs_outer = send(docs.at[2], docs.at[3 - 2 * side], outer)
    docs_after2 = send(docs.at[2], docs.at[0], me + 2)
    docs_before2 = send(docs.at[2], docs.at[4], me - 2)
    kv_after1 = [send(kvw.at[2, g], kvw.at[1, g], me + 1) for g in range(groups)]
    kv_after2 = [send(kvw.at[2, g], kvw.at[0, g], me + 2) for g in range(groups)]
    kv_relay = [send(kvw.at[1, g], kvw.at[0, g], mate) for g in range(groups)]
    gain_send = send(gain, gmate, mate)
    mate_sends = [send(st.at[side, c], mbuf.at[c], mate) for c in range(CHUNKS)]
    outer_sends = [send(cz.at[c], zbuf.at[c], outer) for c in range(CHUNKS)]
    relay_sends = [send(zbuf.at[c], lbuf.at[c], mate) for c in range(CHUNKS)]
    grads_before1 = [send(gs.at[g, 1], gr.at[g, 1], me - 1) for g in range(groups)]
    grads_before2 = [send(gs.at[g, 0], gr.at[g, 0], me - 2) for g in range(groups)]

    ld_load = load(ld_in, ldb)
    doc_load = load(doc_in, docs.at[2])
    sw_load = load(sw_in, srw.at[0])
    sr_load = load(sr_in, srw.at[1])
    x_loads = []
    for c in range(CHUNKS):
        cols = pl.ds(c * chunk_cols, chunk_cols)
        x_loads.append((load(x_in.at[:, cols], xc.at[0, c]), load(cm_in.at[:, cols], xc.at[1, c])))
    kv_loads = []
    for g in range(groups):
        cols = pl.ds(g * HEAD_CHANNELS, HEAD_CHANNELS)
        kv_loads.append((load(k_in.at[:, cols], kvw.at[2, g, 0]), load(v_in.at[:, cols], kvw.at[2, g, 1])))
    q_load = load(q_in, qb)
    do_load = load(do_in, dob)

    barrier = pltpu.get_barrier_semaphore()
    for there, target in (
        (has_before1, me - 1), (has_after1, me + 1), (has_before2, me - 2), (has_after2, me + 2)
    ):
        @pl.when(there)
        def _():
            pl.semaphore_signal(barrier, inc=1, device_id=(target, row), device_id_type=MESH)

    @pl.when(jnp.logical_not(has_before1))
    def _():
        docs[1] = jnp.full(docs.shape[1:], -1, jnp.int32)
        kvw[1] = jnp.zeros(kvw.shape[1:], BF16)

    @pl.when(jnp.logical_not(has_before2))
    def _():
        docs[0] = jnp.full(docs.shape[1:], -1, jnp.int32)

        @pl.when(is_first)
        def _():
            kvw[0] = jnp.zeros(kvw.shape[1:], BF16)

    @pl.when(jnp.logical_not(has_after1))
    def _():
        docs[3] = jnp.full(docs.shape[1:], -1, jnp.int32)
        for g in range(groups):
            gr[g, 1] = jnp.zeros(gr.shape[2:], BF16)

    @pl.when(jnp.logical_not(has_after2))
    def _():
        docs[4] = jnp.full(docs.shape[1:], -1, jnp.int32)
        for g in range(groups):
            gr[g, 0] = jnp.zeros(gr.shape[2:], BF16)

    @pl.when(jnp.logical_not(has_outer))
    def _():
        zbuf[...] = jnp.zeros(zbuf.shape, BF16)

    rows_i = lax.broadcasted_iota(jnp.int32, square, 0)
    cols_i = lax.broadcasted_iota(jnp.int32, square, 1)
    triu = (rows_i <= cols_i).astype(F32)
    ld_load.wait()
    lam_t = dot(ldb[...], triu, precision=lax.Precision.HIGHEST)
    for c in range(CHUNKS):
        lt[c] = lam_t[c * chunk_heads : (c + 1) * chunk_heads]

    spread_at = lax.broadcasted_iota(jnp.int32, (2 * heads, chunk_cols), 0)
    spread_lane = lax.broadcasted_iota(jnp.int32, (2 * heads, chunk_cols), 1)

    def spread(values, slot):
        high = values.astype(BF16)
        low = (values - high.astype(F32)).astype(BF16)
        both = jnp.concatenate([high, low], axis=0)
        for c in range(CHUNKS):
            head = spread_lane // half + c * chunk_heads
            hot = ((spread_at == head) | (spread_at == head + heads)).astype(F32).astype(BF16)
            sc[slot, c] = dot(both, hot, ((0,), (0,)))

    spread(jnp.exp(lam_t[:, tokens - 1 : tokens] - lam_t), 0)
    spread(jnp.exp(lam_t), 1)

    doc_load.wait()
    doc_row = docs[2].astype(F32)
    doc_first = doc_row[:, 0:1]
    doc_last = doc_row[:, tokens - 1 : tokens]
    doc_rows = jnp.broadcast_to(doc_row, square)
    doc_cols = doc_rows.T
    same = doc_rows == doc_cols

    sw_load.wait()
    sr_load.wait()
    writes = srw[0]
    reads = srw[1]
    score = dot(reads, writes, ((1,), (1,)))
    score_t = dot(writes, reads, ((1,), (1,)))
    gmask[0] = jnp.where(same & (rows_i >= cols_i), score, 0.0)
    gmask[1] = jnp.where(same & (cols_i >= rows_i), score_t, 0.0)
    writes_in = jnp.where(doc_cols == doc_last, writes.astype(F32), 0.0)
    reads_in = jnp.where(doc_cols == doc_first, reads.astype(F32), 0.0)
    srw[0] = writes_in.astype(BF16)
    srw[1] = reads_in.astype(BF16)
    srwt[0] = writes_in.T.astype(BF16)
    srwt[1] = reads_in.T.astype(BF16)
    whole = (doc_first == doc_last).astype(F32)
    for c in range(CHUNKS):
        gain[c] = sc[1, c, tokens - 1 : tokens, :] * whole

    for pair in x_loads:
        for copy in pair:
            copy.wait()

    def state(d, c):
        scaled = (xc[d, c].astype(F32) * sc[d, c]).astype(BF16)
        st[d, c] = dot(srwt[d], scaled).astype(BF16)

    for c in range(CHUNKS):
        state(side, c)
    for pair in kv_loads:
        for copy in pair:
            copy.wait()

    pl.semaphore_wait(barrier, has_before1.astype(jnp.int32) + has_before2.astype(jnp.int32) + has_after1.astype(jnp.int32) + has_after2.astype(jnp.int32))

    def start(copies, there=None):
        if there is None:
            for copy in copies:
                copy.start()
        else:
            @pl.when(there)
            def _():
                for copy in copies:
                    copy.start()

    def arrived(copies, there=None):
        if there is None:
            for copy in copies:
                copy.wait_recv()
        else:
            @pl.when(there)
            def _():
                for copy in copies:
                    copy.wait_recv()

    def left(copies, there=None):
        if there is None:
            for copy in copies:
                copy.wait_send()
        else:
            @pl.when(there)
            def _():
                for copy in copies:
                    copy.wait_send()

    start([docs_mate])
    start([docs_outer], has_outer)
    start([docs_after2], has_after2)
    start([docs_before2], has_before2)
    start(kv_after1, has_after1)
    start(kv_after2, has_after2 & is_first)
    start([gain_send] + mate_sends)
    for c in range(CHUNKS):
        state(other, c)

    arrived([docs_mate])
    mate_row = docs[3 - 2 * side].astype(F32)
    mate_first = mate_row[:, 0:1]
    mate_last = mate_row[:, tokens - 1 : tokens]
    joined = jnp.where(is_first, mate_first, mate_last) == jnp.where(is_first, doc_last, doc_first)
    joined = joined.astype(F32)
    for c in range(CHUNKS):
        arrived([mate_sends[c]])
        cz[c] = (st[other, c].astype(F32) + (gain[c] * joined) * mbuf[c].astype(F32)).astype(BF16)
        start([outer_sends[c]], has_outer)

    lane = lax.broadcasted_iota(jnp.int32, (1, 2 * half), 1)
    low_half = (lane < half).astype(F32).astype(BF16)
    high_half = (lane >= half).astype(F32).astype(BF16)

    def inside_block(c, carry):
        for j in range(chunk_heads // 2):
            fwd = []
            bwd = []
            for i in range(2):
                h = 2 * j + i
                lam_rows = jnp.broadcast_to(lt[c, h : h + 1, :], square)
                decay = jnp.exp(-jnp.abs(lam_rows.T - lam_rows))
                fwd.append((decay * gmask[0]).astype(BF16))
                bwd.append((decay * gmask[1]).astype(BF16))
            cols = slice(2 * j * half, (2 * j + 2) * half)
            for d, weights in ((0, fwd), (1, bwd)):
                tile = xc[d, c, :, cols]
                local[d, c, :, cols] = dot(
                    jnp.concatenate(weights, axis=1),
                    jnp.concatenate([tile * low_half, tile * high_half], axis=0),
                )
        return carry

    lax.fori_loop(0, CHUNKS, inside_block, 0)

    arrived([docs_outer], has_outer)
    arrived([docs_after2], has_before2)
    arrived([docs_before2], has_after2)
    q_load.wait()
    do_load.wait()
    minus = -1e30
    for n in range(2):
        before = jnp.broadcast_to(docs[n].astype(F32), square).T
        bias[n * tokens : (n + 1) * tokens] = jnp.where(before == doc_rows, 0.0, minus)
    bias[2 * tokens : 3 * tokens] = jnp.where(same & (cols_i >= rows_i), 0.0, minus)
    for g in range(groups):
        arrived([kv_after1[g]], has_before1)
        start([kv_relay[g]], is_first)
        arrived([kv_after2[g]], has_before2 & is_first)
        arrived([kv_relay[g]], side == 1)
        cols = slice(g * HEAD_CHANNELS, (g + 1) * HEAD_CHANNELS)
        keys = jnp.concatenate([kvw[n, g, 0] for n in range(3)], axis=0)
        values = jnp.concatenate([kvw[n, g, 1] for n in range(3)], axis=0)
        values_t = values.T
        group_heads = range(g * per_group, (g + 1) * per_group)
        for i, h in enumerate(group_heads):
            hcols = slice(h * HEAD_CHANNELS, (h + 1) * HEAD_CHANNELS)
            icols = slice(i * tokens, (i + 1) * tokens)
            raw = dot(keys, qb[:, hcols], ((1,), (1,))) + bias[...]
            peak = jnp.max(raw, axis=0, keepdims=True)
            raised = jnp.exp((raw - peak) * inv_root)
            probs = (raised * (1.0 / jnp.sum(raised, axis=0, keepdims=True))).astype(BF16)
            pt[:, icols] = probs
            ao[:, hcols] = dot(values_t, probs).T.astype(BF16)
            prob_grad = dot(values, dob[:, hcols], ((1,), (1,)))
            single = probs.astype(F32)
            inner = jnp.sum(single * prob_grad, axis=0, keepdims=True)
            dst[:, icols] = (single * (prob_grad - inner) * inv_root).astype(BF16)
        q_rows, do_rows = (
            jnp.concatenate([ref[:, h * HEAD_CHANNELS : (h + 1) * HEAD_CHANNELS] for h in group_heads], axis=0)
            for ref in (qb, dob)
        )
        for n, grad in enumerate((dot(dst[...], q_rows), dot(pt[...], do_rows))):
            gs[g, 0, n] = grad[0:tokens].astype(BF16)
            gs[g, 1, n] = grad[tokens : 2 * tokens].astype(BF16)
            gown[n, :, cols] = grad[2 * tokens :]
        start([grads_before1[g]], has_before1)
        start([grads_before2[g]], has_before2)

    for c in range(CHUNKS):
        arrived([outer_sends[c]], has_outer)
        start([relay_sends[c]])

    outer_row = docs[1 + 2 * side].astype(F32)
    far_row = docs[4 - 4 * side].astype(F32)
    outer_joined = jnp.where(is_first, outer_row[:, tokens - 1 : tokens], outer_row[:, 0:1]) == jnp.where(
        is_first, doc_first, doc_last
    )
    mate_joined = jnp.where(is_first, mate_last, mate_first) == jnp.where(
        is_first, far_row[:, 0:1], far_row[:, tokens - 1 : tokens]
    )
    mate_joined = mate_joined.astype(F32)

    def finish(d, c, rows, carried):
        cols = slice(c * chunk_cols, (c + 1) * chunk_cols)
        mix[d, :, cols] = (local[d, c] + sc[1 - d, c] * dot(rows, carried)).astype(BF16)

    rows = (srw[other].astype(F32) * outer_joined.astype(F32)).astype(BF16)
    for c in range(CHUNKS):
        finish(side, c, rows, zbuf[c])
    rows = (srw[side].astype(F32) * joined).astype(BF16)
    arrived([gain_send])
    for c in range(CHUNKS):
        arrived([relay_sends[c]])
        carried = mbuf[c].astype(F32) + (gmate[c] * mate_joined) * lbuf[c].astype(F32)
        finish(other, c, rows, carried.astype(BF16))

    arrived(grads_before1, has_after1)
    arrived(grads_before2, has_after2)
    for n in range(2):
        for g in range(groups):
            cols = slice(g * HEAD_CHANNELS, (g + 1) * HEAD_CHANNELS)
            total = gown[n, :, cols] + gr[g, 1, n].astype(F32) + gr[g, 0, n].astype(F32)
            gkv[n, :, cols] = total.astype(BF16)

    left([docs_mate, gain_send] + mate_sends + relay_sends)
    left([docs_outer] + outer_sends, has_outer)
    left([docs_after2], has_after2)
    left([docs_before2] + grads_before2, has_before2)
    left(kv_after1, has_after1)
    left(kv_after2, has_after2 & is_first)
    left(kv_relay, is_first)
    left(grads_before1, has_before1)


def store_kernel(ao, mix, gkv, ao_out, mo_out, gk_out, gv_out, gx_out, sem):
    copies = [
        pltpu.make_async_copy(src, dst, sem.at[n])
        for n, (src, dst) in enumerate(
            ((mix.at[0], mo_out), (mix.at[1], gx_out), (ao, ao_out), (gkv.at[0], gk_out), (gkv.at[1], gv_out))
        )
    ]
    for copy in copies:
        copy.start()
    for copy in copies:
        copy.wait()


def shards(q, k, v, x, ld, sw, sr, doc, do, cm):
    tokens = q.shape[0]
    groups = k.shape[1] // HEAD_CHANNELS
    per_group = q.shape[1] // k.shape[1]
    heads = ld.shape[1]
    states = sw.shape[1]
    chunk_cols = x.shape[1] // CHUNKS
    span = 3 * tokens
    remotes = 4 + 3 * groups + 1 + 3 * CHUNKS + 2 * groups
    locals_ = 4 + 2 * CHUNKS + 2 * groups + 2
    vmem = pltpu.VMEM
    hbm = pl.BlockSpec(memory_space=pltpu.HBM)
    onchip = pl.BlockSpec(memory_space=pltpu.VMEM)
    shape = jax.ShapeDtypeStruct
    operands = [
        pltpu.with_memory_space_constraint(a, pltpu.HBM) for a in (q, k, v, x, ld.T, sw, sr, doc.reshape(1, tokens), do, cm)
    ]
    parts = pl.pallas_call(
        step_kernel,
        out_shape=(shape(q.shape, BF16), shape((2,) + x.shape, BF16), shape((2,) + k.shape, BF16)),
        in_specs=[hbm] * 10,
        out_specs=[onchip] * 3,
        scratch_shapes=[
            vmem(q.shape, BF16),
            vmem(q.shape, BF16),
            vmem((2, CHUNKS, tokens, chunk_cols), BF16),
            vmem((heads, tokens), F32),
            vmem((2, tokens, states), BF16),
            vmem((2, states, tokens), BF16),
            vmem((5, 1, tokens), jnp.int32),
            vmem((3, groups, 2, tokens, HEAD_CHANNELS), BF16),
            vmem((2, CHUNKS, tokens, chunk_cols), F32),
            vmem((CHUNKS, heads // CHUNKS, tokens), F32),
            vmem((2, CHUNKS, states, chunk_cols), BF16),
            vmem((CHUNKS, states, chunk_cols), BF16),
            vmem((CHUNKS, states, chunk_cols), BF16),
            vmem((CHUNKS, states, chunk_cols), BF16),
            vmem((CHUNKS, states, chunk_cols), BF16),
            vmem((CHUNKS, 1, chunk_cols), F32),
            vmem((CHUNKS, 1, chunk_cols), F32),
            vmem((2, CHUNKS, tokens, chunk_cols), F32),
            vmem((span, per_group * tokens), BF16),
            vmem((span, per_group * tokens), BF16),
            vmem((span, tokens), F32),
            vmem((groups, 2, 2, tokens, HEAD_CHANNELS), BF16),
            vmem((groups, 2, 2, tokens, HEAD_CHANNELS), BF16),
            vmem((2,) + k.shape, F32),
            vmem((2, tokens, tokens), F32),
            pltpu.SemaphoreType.DMA((locals_,)),
            pltpu.SemaphoreType.DMA((remotes,)),
            pltpu.SemaphoreType.DMA((remotes,)),
        ],
        compiler_params=pltpu.CompilerParams(collective_id=0, has_side_effects=True, vmem_limit_bytes=40 << 20),
        name="step",
    )(*operands)
    return pl.pallas_call(
        store_kernel,
        out_shape=(
            shape(q.shape, BF16), shape(x.shape, BF16), shape(k.shape, BF16), shape(v.shape, BF16), shape(x.shape, BF16),
        ),
        in_specs=[onchip] * 3,
        out_specs=[hbm] * 5,
        scratch_shapes=[pltpu.SemaphoreType.DMA((5,))],
        compiler_params=pltpu.CompilerParams(vmem_limit_bytes=8 << 20),
        name="store",
    )(*parts)


def solution(mesh):
    both = P("ctx", "tp")
    return jax.shard_map(
        shards,
        mesh=mesh,
        in_specs=(both, both, both, both, both, P("ctx", None), P("ctx", None), P("ctx"), both, both),
        out_specs=(both,) * 5,
        check_vma=False,
    )
```

```python
import math

import jax
import jax.numpy as jnp
from jax import lax
from jax.experimental import pallas as pl
from jax.experimental.pallas import tpu as pltpu
from jax.sharding import PartitionSpec as P

HEAD_CHANNELS = 128
CHUNKS = 4
ROUND = 16
MESH = pl.DeviceIdType.MESH
F32 = jnp.float32
BF16 = jnp.bfloat16


def dot(a, b, contract=((1,), (0,))):
    return lax.dot_general(a, b, (contract, ((), ())), preferred_element_type=F32)


def bf16_parts(values, count):
    parts = []
    for _ in range(count):
        parts.append(values.astype(BF16))
        values = values - parts[-1].astype(F32)
    return jnp.concatenate(parts, axis=0)


def step_kernel(
    q_in, k_in, v_in, x_in, ld_in, sw_in, sr_in, doc_in, do_in, cm_in,
    ao, mix, gkv,
    qw, dow, xc, ldb, srw, srwt, docs, kvo, kvw, scale, wrow, sc, lt, st, mbuf, cz, zbuf, lbuf, gain, gmate,
    local, pt, dst, bias, aob, aom, gs, gacc, gr, gsm, grm, gmask, lsem, ssem, rsem,
):
    tokens = qw.shape[1]
    wide = qw.shape[2]
    heads = ld_in.shape[0]
    per_group = wide // HEAD_CHANNELS
    chunk_cols = x_in.shape[1] // CHUNKS
    chunk_heads = heads // CHUNKS
    half = chunk_cols // chunk_heads
    inv_root = 1.0 / math.sqrt(HEAD_CHANNELS)
    square = (tokens, tokens)

    count = lax.axis_size("ctx")
    me = lax.axis_index("ctx")
    row = lax.axis_index("tp")
    side = lax.rem(me, 2)
    other = 1 - side
    own = 2 + side
    mate = me + 1 - 2 * side
    outer = me - 1 + 2 * side
    before = [me - side - 2, me - side - 1]
    after = [me - side + 2, me - side + 3]
    has_before = me >= 2
    has_after = me < count - 2
    is_first = side == 0
    has_outer = (is_first & has_before) | (jnp.logical_not(is_first) & has_after)

    local_at = [0]

    def load(src, dst_ref):
        copy = pltpu.make_async_copy(src, dst_ref, lsem.at[local_at[0]])
        local_at[0] += 1
        copy.start()
        return copy

    send_at = [0]
    recv_at = [0]

    def slot(at, n=1):
        at[0] += n
        return at[0] - n

    def copy_to(src, dst_ref, target, recv):
        return pltpu.make_async_remote_copy(
            src_ref=src, dst_ref=dst_ref, send_sem=ssem.at[slot(send_at)], recv_sem=rsem.at[recv],
            device_id=(target, row), device_id_type=MESH,
        )

    def send(src, dst_ref, target):
        return copy_to(src, dst_ref, target, slot(recv_at))

    def each(copies, act, there):
        if there is None:
            for copy in copies:
                act(copy)
        else:
            @pl.when(there)
            def _():
                for copy in copies:
                    act(copy)

    def start(copies, there=None):
        each(copies, lambda copy: copy.start(), there)

    def arrived(copies, there=None):
        each(copies, lambda copy: copy.wait_recv(), there)

    def left(copies, there=None):
        each(copies, lambda copy: copy.wait_send(), there)

    def over(count, body):
        lax.fori_loop(0, count, lambda c, carry: (body(c), carry)[1], 0)

    def part(which, width):
        return pl.ds(pl.multiple_of(which * width, width), width)

    docs_mate = send(docs.at[own], docs.at[own], mate)
    at = slot(recv_at, 2)
    docs_after = [copy_to(docs.at[own], docs.at[side], after[h], at + side) for h in range(2)]
    docs_from = [copy_to(docs.at[own], docs.at[h], mate, at + h) for h in range(2)]
    at = slot(recv_at)
    docs_before = [copy_to(docs.at[2], docs.at[4], before[h], at) for h in range(2)]
    kv_mate = send(kvo.at[other], kvw.at[own], mate)
    at = slot(recv_at, 2)
    kv_after = [copy_to(kvo.at[h], kvw.at[side], after[h], at + side) for h in range(2)]
    kv_from = [copy_to(kvo.at[h], kvw.at[h], mate, at + h) for h in range(2)]
    q_mate = send(q_in.at[:, part(other, wide)], qw.at[side], mate)
    do_mate = send(do_in.at[:, part(other, wide)], dow.at[side], mate)
    gain_send = send(gain, gmate, mate)

    def chunked(src, dst_ref, target):
        base_send, base_recv = slot(send_at, CHUNKS), slot(recv_at, CHUNKS)

        def copy(c):
            return pltpu.make_async_remote_copy(
                src_ref=src.at[c], dst_ref=dst_ref.at[c], send_sem=ssem.at[base_send + c], recv_sem=rsem.at[base_recv + c],
                device_id=(target, row), device_id_type=MESH,
            )

        return copy

    mate_send = chunked(st.at[side], mbuf, mate)
    outer_send = chunked(cz, zbuf, outer)
    relay_send = chunked(zbuf, lbuf, mate)
    ao_mate = send(aob.at[other], aom, mate)
    at = slot(recv_at, 2)
    grads_at = slot(send_at, 2)

    def grads_before(h):
        return pltpu.make_async_remote_copy(
            src_ref=gs.at[h], dst_ref=gr.at[side], send_sem=ssem.at[grads_at + h], recv_sem=rsem.at[at + side],
            device_id=(before[0] + h, row), device_id_type=MESH,
        )

    grads_from = [copy_to(gs.at[h], gr.at[h], mate, at + h) for h in range(2)]
    grads_mate = send(gsm, grm, mate)

    barrier = pltpu.get_barrier_semaphore()
    for there, targets in ((None, [mate]), (has_before, before), (has_after, after)):
        each(
            targets,
            lambda target: pl.semaphore_signal(barrier, inc=1, device_id=(target, row), device_id_type=MESH),
            there,
        )

    doc_load = load(doc_in, docs.at[own])
    kv_loads = []
    for h in range(2):
        cols = pl.ds(h * HEAD_CHANNELS, HEAD_CHANNELS)
        kv_loads += [load(k_in.at[:, cols], kvo.at[h, 0]), load(v_in.at[:, cols], kvo.at[h, 1])]
    ld_load = load(ld_in, ldb)
    sw_load = load(sw_in, srw.at[0])
    sr_load = load(sr_in, srw.at[1])
    x_at = local_at[0]
    local_at[0] += 2
    for d, src in enumerate((x_in, cm_in)):
        for c in range(CHUNKS):
            pltpu.make_async_copy(src.at[:, pl.ds(c * chunk_cols, chunk_cols)], xc.at[d, c], lsem.at[x_at + d]).start()
    own_loads = [
        load(k_in.at[:, part(side, HEAD_CHANNELS)], kvw.at[own, 0]),
        load(v_in.at[:, part(side, HEAD_CHANNELS)], kvw.at[own, 1]),
        load(q_in.at[:, part(side, wide)], qw.at[side]),
        load(do_in.at[:, part(side, wide)], dow.at[side]),
    ]

    @pl.when(jnp.logical_not(has_before))
    def _():
        for h in range(2):
            docs[h] = jnp.full(docs.shape[1:], -1, jnp.int32)
            kvw[h] = jnp.zeros(kvw.shape[1:], BF16)

    @pl.when(jnp.logical_not(has_after))
    def _():
        docs[4] = jnp.full(docs.shape[1:], -1, jnp.int32)
        gr[...] = jnp.zeros(gr.shape, BF16)

    @pl.when(jnp.logical_not(has_outer))
    def _():
        zbuf[...] = jnp.zeros(zbuf.shape, BF16)

    def announce():
        pl.semaphore_wait(barrier, 1 + 2 * has_before.astype(jnp.int32) + 2 * has_after.astype(jnp.int32))
        start([docs_mate])
        start(docs_after + kv_after, has_after)
        start(docs_before, has_before & is_first)
        start([kv_mate, q_mate, do_mate])

    sends_early = lax.rem(me, ROUND) >= ROUND // 2
    doc_load.wait()
    for copy in kv_loads:
        copy.wait()

    @pl.when(sends_early)
    def _():
        announce()

    rows_i = lax.broadcasted_iota(jnp.int32, square, 0)
    cols_i = lax.broadcasted_iota(jnp.int32, square, 1)
    triu = (rows_i <= cols_i).astype(F32).astype(BF16)
    ld_load.wait()
    sums = dot(bf16_parts(ldb[...], 3), triu)
    lam_t = (sums[2 * heads :] + sums[heads : 2 * heads]) + sums[:heads]
    for c in range(CHUNKS):
        lt[c] = lam_t[c * chunk_heads : (c + 1) * chunk_heads]
    exits = jnp.exp(lam_t[:, tokens - 1 : tokens] - lam_t)
    entries = jnp.exp(lam_t)
    for c in range(CHUNKS):
        wrow[0, c] = exits[c * chunk_heads : (c + 1) * chunk_heads]
        wrow[1, c] = entries[c * chunk_heads : (c + 1) * chunk_heads]

    doc_row = docs[own].astype(F32)
    doc_first = doc_row[:, 0:1]
    doc_last = doc_row[:, tokens - 1 : tokens]
    doc_rows = jnp.broadcast_to(doc_row, square)
    doc_cols = doc_rows.T
    sw_load.wait()
    sr_load.wait()
    writes = srw[0]
    reads = srw[1]
    writes_in = jnp.where(doc_cols == doc_last, writes.astype(F32), 0.0)
    reads_in = jnp.where(doc_cols == doc_first, reads.astype(F32), 0.0)
    srw[0] = writes_in.astype(BF16)
    srw[1] = reads_in.astype(BF16)
    srwt[0] = writes_in.T
    srwt[1] = reads_in.T

    lane = lax.broadcasted_iota(jnp.int32, (1, 2 * half), 1)
    low_half = (lane < half).astype(F32).astype(BF16)
    high_half = (lane >= half).astype(F32).astype(BF16)

    def two_heads(tile):
        return jnp.concatenate([tile * low_half, tile * high_half], axis=0)

    def state(d, c):
        weights = wrow[d, c]
        for j in range(chunk_heads // 2):
            cols = slice(2 * j * half, (2 * j + 2) * half)
            left_side = [(srwt[d] * weights[h : h + 1]).astype(BF16) for h in (2 * j, 2 * j + 1)]
            st[d, c, :, cols] = dot(jnp.concatenate(left_side, axis=1), two_heads(xc[d, c, :, cols])).astype(BF16)

    for d in range(2):
        pltpu.make_async_copy(xc.at[d], xc.at[d], lsem.at[x_at + d]).wait()

    def first_state(c):
        state(side, c)
        start([mate_send(c)], sends_early)

    over(CHUNKS, first_state)

    @pl.when(jnp.logical_not(sends_early))
    def _():
        announce()
        over(CHUNKS, lambda c: mate_send(c).start())

    over(CHUNKS, lambda c: state(other, c))

    whole = (doc_first == doc_last).astype(F32)

    def gains(c):
        ends = wrow[1, c][:, tokens - 1 : tokens] * whole
        pairs = [
            jnp.where(lane < half, ends[h : h + 1], ends[h + 1 : h + 2]) for h in range(0, chunk_heads, 2)
        ]
        gain[c] = jnp.concatenate(pairs, axis=1)

    over(CHUNKS, gains)
    start([gain_send])

    def edge(early, late):
        ends = docs[early].astype(F32)[:, tokens - 1 : tokens]
        return (docs[late].astype(F32)[:, 0:1] == ends).astype(F32)

    arrived([docs_mate])
    joined = edge(2, 3)

    def combine(c):
        mate_send(c).wait_recv()
        cz[c] = (st[other, c].astype(F32) + (gain[c] * joined) * mbuf[c].astype(F32)).astype(BF16)
        start([outer_send(c)], has_outer)

    over(CHUNKS, combine)

    scale[0] = bf16_parts(exits, 2).T
    scale[1] = bf16_parts(entries, 2).T
    spread_at = lax.broadcasted_iota(jnp.int32, (2 * heads, chunk_cols), 0)
    spread_head = lax.broadcasted_iota(jnp.int32, (2 * heads, chunk_cols), 1) // half

    same = doc_rows == doc_cols
    gmask[0] = jnp.where(same & (rows_i >= cols_i), dot(reads, writes, ((1,), (1,))), 0.0)
    gmask[1] = jnp.where(same & (cols_i >= rows_i), dot(writes, reads, ((1,), (1,))), 0.0)

    def inside_block(c):
        head = spread_head + c * chunk_heads
        hot = ((spread_at == head) | (spread_at == head + heads)).astype(F32).astype(BF16)
        for d in range(2):
            sc[d, c] = dot(scale[d], hot)
        for j in range(chunk_heads // 2):
            fwd = []
            bwd = []
            for h in (2 * j, 2 * j + 1):
                lam_rows = jnp.broadcast_to(lt[c, h : h + 1, :], square)
                decay = jnp.exp(-jnp.abs(lam_rows.T - lam_rows))
                fwd.append((decay * gmask[0]).astype(BF16))
                bwd.append((decay * gmask[1]).astype(BF16))
            cols = slice(2 * j * half, (2 * j + 2) * half)
            for d, weights in ((0, fwd), (1, bwd)):
                local[d, c, :, cols] = dot(jnp.concatenate(weights, axis=1), two_heads(xc[d, c, :, cols]))

    over(CHUNKS, inside_block)

    arrived(docs_from, has_before)
    for copy in own_loads:
        copy.wait()
    arrived([q_mate, do_mate, kv_mate])
    arrived(kv_from, has_before)
    gacc[...] = jnp.zeros(gacc.shape, F32)

    def attend(pos):
        rows = jnp.broadcast_to(docs[2 + pos].astype(F32), square)
        for n in range(3):
            keep = jnp.broadcast_to(docs[pos + n].astype(F32), square).T == rows
            if n == 2:
                keep = keep & (cols_i >= rows_i)
            bias[n * tokens : (n + 1) * tokens] = jnp.where(keep, 0.0, -1e30)

        def two_queries(pair):
            def pair_of(ref):
                return jnp.concatenate(
                    [ref[pos, :, pl.ds(pl.multiple_of((2 * pair + i) * HEAD_CHANNELS, HEAD_CHANNELS), HEAD_CHANNELS)] for i in range(2)],
                    axis=0,
                )

            keys = jnp.concatenate([kvw[pos + n, 0] for n in range(3)], axis=0)
            values = jnp.concatenate([kvw[pos + n, 1] for n in range(3)], axis=0)
            mask = jnp.concatenate([bias[...], bias[...]], axis=1)
            raw = dot(keys, pair_of(qw), ((1,), (1,))) + mask
            peak = jnp.max(raw, axis=0, keepdims=True)
            raised = jnp.exp((raw - peak) * inv_root)
            probs = (raised * (1.0 / jnp.sum(raised, axis=0, keepdims=True))).astype(BF16)
            pt[pair] = probs
            out_t = dot(values.T, probs)
            for i in range(2):
                cols = pl.ds(pl.multiple_of((2 * pair + i) * HEAD_CHANNELS, HEAD_CHANNELS), HEAD_CHANNELS)
                aob[pos, :, cols] = out_t[:, i * tokens : (i + 1) * tokens].T.astype(BF16)
            prob_grad = dot(values, pair_of(dow), ((1,), (1,)))
            single = probs.astype(F32)
            inner = jnp.sum(single * prob_grad, axis=0, keepdims=True)
            dst[pair] = (single * (prob_grad - inner) * inv_root).astype(BF16)

        over(per_group // 2, two_queries)
        for n, (probs_ref, rows_ref) in enumerate(((dst, qw), (pt, dow))):
            grad = dot(
                jnp.concatenate([probs_ref[pair] for pair in range(per_group // 2)], axis=1),
                jnp.concatenate(
                    [rows_ref[pos, :, i * HEAD_CHANNELS : (i + 1) * HEAD_CHANNELS] for i in range(per_group)], axis=0
                ),
            )
            for m in range(3):
                gacc[pos + m, n] += grad[m * tokens : (m + 1) * tokens]
            gs[pos, n] = gacc[pos, n].astype(BF16)
        start([grads_before(pos)], has_before)

    over(2, attend)
    start([ao_mate])
    for n in range(2):
        gsm[n] = gacc[2 + other, n].astype(BF16)
    start([grads_mate])
    ao[side] = aob[side]

    arrived([docs_before[0]], has_after)
    in_before = edge(1, 2)
    in_after = edge(3, 4)
    outer_joined = jnp.where(is_first, in_before, in_after)
    mate_joined = jnp.where(is_first, in_after, in_before)

    def finish(d, c, rows, carried):
        mix[d, :, part(c, chunk_cols)] = (local[d, c] + sc[1 - d, c] * dot(rows, carried)).astype(BF16)

    rows = (srw[other].astype(F32) * outer_joined).astype(BF16)

    def from_outside(c):
        arrived([outer_send(c)], has_outer)
        relay_send(c).start()
        finish(side, c, rows, zbuf[c])

    over(CHUNKS, from_outside)
    mate_rows = (srw[side].astype(F32) * joined).astype(BF16)
    arrived([gain_send])

    def from_mate(c):
        relay_send(c).wait_recv()
        carried = mbuf[c].astype(F32) + (gmate[c] * mate_joined) * lbuf[c].astype(F32)
        finish(other, c, mate_rows, carried.astype(BF16))


    left([docs_mate, kv_mate, q_mate, do_mate, gain_send])
    left(docs_after + kv_after, has_after)
    left(docs_before, has_before & is_first)

    def carries_left(c):
        mate_send(c).wait_send()
        left([outer_send(c)], has_outer)

    over(CHUNKS, carries_left)
    over(CHUNKS, from_mate)

    arrived([ao_mate, grads_mate])
    ao[other] = aom[...]
    arrived(grads_from, has_after)
    for n in range(2):
        gkv[side, n] = (gacc[own, n] + gr[side, n].astype(F32)).astype(BF16)
        gkv[other, n] = (grm[n].astype(F32) + gr[other, n].astype(F32)).astype(BF16)

    left([ao_mate, grads_mate])
    left([grads_before(0), grads_before(1)], has_before)
    over(CHUNKS, lambda c: relay_send(c).wait_send())


def store_kernel(ao, mix, gkv, ao_out, mo_out, gk_out, gv_out, gx_out, sem):
    moves = [(mix.at[0], mo_out), (mix.at[1], gx_out)]
    for h in range(2):
        wide = ao.shape[2]
        moves.append((ao.at[h], ao_out.at[:, pl.ds(h * wide, wide)]))
        for n, out in enumerate((gk_out, gv_out)):
            moves.append((gkv.at[h, n], out.at[:, pl.ds(h * HEAD_CHANNELS, HEAD_CHANNELS)]))
    copies = [pltpu.make_async_copy(src, dst, sem.at[n]) for n, (src, dst) in enumerate(moves)]
    for copy in copies:
        copy.start()
    for copy in copies:
        copy.wait()


def shards(q, k, v, x, ld, sw, sr, doc, do, cm):
    tokens = q.shape[0]
    assert k.shape[1] == 2 * HEAD_CHANNELS
    wide = q.shape[1] // 2
    heads = ld.shape[1]
    states = sw.shape[1]
    chunk_cols = x.shape[1] // CHUNKS
    span = 3 * tokens
    square = (tokens, HEAD_CHANNELS)
    vmem = pltpu.VMEM
    hbm = pl.BlockSpec(memory_space=pltpu.HBM)
    onchip = pl.BlockSpec(memory_space=pltpu.VMEM)
    shape = jax.ShapeDtypeStruct
    operands = [
        pltpu.with_memory_space_constraint(a, pltpu.HBM) for a in (q, k, v, x, ld.T, sw, sr, doc.reshape(1, tokens), do, cm)
    ]
    parts = pl.pallas_call(
        step_kernel,
        out_shape=(shape((2, tokens, wide), BF16), shape((2,) + x.shape, BF16), shape((2, 2) + square, BF16)),
        in_specs=[hbm] * 10,
        out_specs=[onchip] * 3,
        scratch_shapes=[
            vmem((2, tokens, wide), BF16),
            vmem((2, tokens, wide), BF16),
            vmem((2, CHUNKS, tokens, chunk_cols), BF16),
            vmem((heads, tokens), F32),
            vmem((2, tokens, states), BF16),
            vmem((2, states, tokens), F32),
            vmem((5, 1, tokens), jnp.int32),
            vmem((2, 2) + square, BF16),
            vmem((4, 2) + square, BF16),
            vmem((2, tokens, 2 * heads), BF16),
            vmem((2, CHUNKS, heads // CHUNKS, tokens), F32),
            vmem((2, CHUNKS, tokens, chunk_cols), F32),
            vmem((CHUNKS, heads // CHUNKS, tokens), F32),
            vmem((2, CHUNKS, states, chunk_cols), BF16),
            vmem((CHUNKS, states, chunk_cols), BF16),
            vmem((CHUNKS, states, chunk_cols), BF16),
            vmem((CHUNKS, states, chunk_cols), BF16),
            vmem((CHUNKS, states, chunk_cols), BF16),
            vmem((CHUNKS, 1, chunk_cols), F32),
            vmem((CHUNKS, 1, chunk_cols), F32),
            vmem((2, CHUNKS, tokens, chunk_cols), F32),
            vmem((wide // HEAD_CHANNELS // 2, span, 2 * tokens), BF16),
            vmem((wide // HEAD_CHANNELS // 2, span, 2 * tokens), BF16),
            vmem((span, tokens), F32),
            vmem((2, tokens, wide), BF16),
            vmem((tokens, wide), BF16),
            vmem((2, 2) + square, BF16),
            vmem((4, 2) + square, F32),
            vmem((2, 2) + square, BF16),
            vmem((2,) + square, BF16),
            vmem((2,) + square, BF16),
            vmem((2, tokens, tokens), F32),
            pltpu.SemaphoreType.DMA((14,)),
            pltpu.SemaphoreType.DMA((21 + 3 * CHUNKS,)),
            pltpu.SemaphoreType.DMA((14 + 3 * CHUNKS,)),
        ],
        compiler_params=pltpu.CompilerParams(collective_id=0, has_side_effects=True, vmem_limit_bytes=40 << 20),
        name="step",
    )(*operands)
    return pl.pallas_call(
        store_kernel,
        out_shape=(
            shape(q.shape, BF16), shape(x.shape, BF16), shape(k.shape, BF16), shape(v.shape, BF16), shape(x.shape, BF16),
        ),
        in_specs=[onchip] * 3,
        out_specs=[hbm] * 5,
        scratch_shapes=[pltpu.SemaphoreType.DMA((8,))],
        compiler_params=pltpu.CompilerParams(vmem_limit_bytes=8 << 20),
        name="store",
    )(*parts)


def solution(mesh):
    both = P("ctx", "tp")
    return jax.shard_map(
        shards,
        mesh=mesh,
        in_specs=(both, both, both, both, both, P("ctx", None), P("ctx", None), P("ctx"), both, both),
        out_specs=(both,) * 5,
        check_vma=False,
    )
```

```python
import math

import jax
import jax.numpy as jnp
from jax import lax
from jax.experimental import pallas as pl
from jax.experimental.pallas import tpu as pltpu
from jax.sharding import PartitionSpec as P

HEAD_CHANNELS = 128
CHUNKS = 4
DOUBLED = 128
ROUND = 16
MESH = pl.DeviceIdType.MESH
F32 = jnp.float32
BF16 = jnp.bfloat16


def dot(a, b, contract=((1,), (0,))):
    return lax.dot_general(a, b, (contract, ((), ())), preferred_element_type=F32)


def bf16_parts(values, count):
    parts = []
    for _ in range(count):
        parts.append(values.astype(BF16))
        values = values - parts[-1].astype(F32)
    return jnp.concatenate(parts, axis=0)


def step_kernel(
    q_in, k_in, v_in, x_in, ld_in, sw_in, sr_in, doc_in, do_in, cm_in,
    ao, mix, gkv,
    qw, dow, xc, ldb, srw, srwt, docs, kvo, kvw, scale, wrow, sc, lt, st, mbuf, cz, zbuf, lbuf, gain, gmate,
    local, pt, dst, bias, aob, aom, gs, gacc, gr, gsm, grm, gmask, lsem, ssem, rsem, ready,
):
    tokens = qw.shape[1]
    wide = qw.shape[2]
    heads = ld_in.shape[0]
    per_group = wide // HEAD_CHANNELS
    chunk_cols = x_in.shape[1] // CHUNKS
    chunk_heads = heads // CHUNKS
    half = chunk_cols // chunk_heads
    inv_root = 1.0 / math.sqrt(HEAD_CHANNELS)
    square = (tokens, tokens)

    count = lax.axis_size("ctx")
    me = lax.axis_index("ctx")
    row = lax.axis_index("tp")
    side = lax.rem(me, 2)
    other = 1 - side
    own = 2 + side
    mate = me + 1 - 2 * side
    outer = me - 1 + 2 * side
    before = [me - side - 2, me - side - 1]
    after = [me - side + 2, me - side + 3]
    has_before = me >= 2
    has_after = me < count - 2
    is_first = side == 0
    at_front = has_before & (lax.rem(me, ROUND) < 2)
    at_back = has_after & (lax.rem(me, ROUND) >= ROUND - 2)
    has_outer = (is_first & has_before) | (jnp.logical_not(is_first) & has_after)

    sems = {}

    def sem(kind, name, width=1):
        ref, used = {"local": (lsem, 0), "send": (ssem, 1), "recv": (rsem, 2)}[kind]
        if (kind, name) not in sems:
            sems[kind, name] = sems.get(used, 0)
            sems[used] = sems.get(used, 0) + width
        return ref, sems[kind, name]

    def drain(kind, name, ref, at=0):
        array, first = sem(kind, name)
        pltpu.make_async_copy(ref, ref, array.at[first + at]).wait()

    def load(name, src, dst_ref):
        array, first = sem("local", name)
        pltpu.make_async_copy(src, dst_ref, array.at[first]).start()

    def send(name, src, dst_ref, target, at=0, width=1):
        out, out_first = sem("send", name)
        into, into_first = sem("recv", name, width)
        return pltpu.make_async_remote_copy(
            src_ref=src, dst_ref=dst_ref, send_sem=out.at[out_first], recv_sem=into.at[into_first + at],
            device_id=(target, row), device_id_type=MESH,
        )

    def each(copies, act, there):
        if there is None:
            for copy in copies:
                act(copy)
        else:
            @pl.when(there)
            def _():
                for copy in copies:
                    act(copy)

    def start(copies, there=None):
        each(copies, lambda copy: copy.start(), there)

    def drained(kind, waits, there=None):
        each(waits, lambda wait: drain(kind, *wait), there)

    def over(count, body):
        lax.fori_loop(0, count, lambda c, carry: (body(c), carry)[1], 0)

    def part(which, width):
        return pl.ds(pl.multiple_of(which * width, width), width)

    docs_mate = send("docs_mate", docs.at[own], docs.at[own], mate)
    docs_after = [send("docs_after", docs.at[own], docs.at[side], after[h]) for h in range(2)]
    docs_before = [send("docs_before", docs.at[2], docs.at[4], before[h]) for h in range(2)]
    kv_mate = send("kv_mate", kvo.at[other], kvw.at[own], mate)
    kv_after = [send("kv_after", kvo.at[h], kvw.at[side], after[h]) for h in range(2)]
    q_mate = send("q_mate", q_in.at[:, part(other, wide)], qw.at[side], mate)
    do_mate = send("q_mate", do_in.at[:, part(other, wide)], dow.at[side], mate)
    gain_send = send("gain", gain, gmate, mate)
    ao_mate = send("ao", aob.at[other], aom, mate)
    grads_mate = send("grads_mate", gsm, grm, mate)
    sem("recv", "mate", CHUNKS)
    sem("recv", "outer", CHUNKS)
    sem("recv", "relay", CHUNKS)

    def grads_before(h):
        return send("grads", gs.at[h], gr.at[side], before[0] + h)

    def mate_send(c):
        return send("mate", st.at[side, c], mbuf.at[c], mate, c)

    def outer_send(c):
        return send("outer", cz.at[c], zbuf.at[c], outer, c)

    def relay_send(c):
        return send("relay", zbuf.at[c], lbuf.at[c], mate, c)

    last = CHUNKS - 1
    halves = [pl.ds(0, chunk_cols - DOUBLED), pl.ds(chunk_cols - DOUBLED, DOUBLED)]
    low_send = send("low", cz.at[last, :, halves[0]], zbuf.at[last, :, halves[0]], outer)
    high_send = send("high", cz.at[last, :, halves[1]], zbuf.at[last, :, halves[1]], outer)
    far_send = send("far", cz.at[last, :, halves[1]], lbuf.at[last, :, halves[1]], outer - 1 + 2 * side)
    low_relay = send("low_relay", zbuf.at[last, :, halves[0]], lbuf.at[last, :, halves[0]], mate)

    barrier = pltpu.get_barrier_semaphore()

    def tell(semaphore, targets, there=None):
        each(
            targets,
            lambda target: pl.semaphore_signal(semaphore, inc=1, device_id=(target, row), device_id_type=MESH),
            there,
        )

    tell(barrier, [mate])
    tell(barrier, before, has_before)
    tell(barrier, after, has_after & jnp.logical_not(at_back))

    load("doc", doc_in, docs.at[own])
    for h in range(2):
        cols = pl.ds(h * HEAD_CHANNELS, HEAD_CHANNELS)
        load("kv", k_in.at[:, cols], kvo.at[h, 0])
        load("kv", v_in.at[:, cols], kvo.at[h, 1])
    load("ld", ld_in, ldb)
    load("states", sw_in, srw.at[0])
    load("states", sr_in, srw.at[1])
    for d, src in enumerate((x_in, cm_in)):
        for c in range(CHUNKS):
            load("x", src.at[:, pl.ds(c * chunk_cols, chunk_cols)], xc.at[d, c])
    load("own_kv", k_in.at[:, part(side, HEAD_CHANNELS)], kvw.at[own, 0])
    load("own_kv", v_in.at[:, part(side, HEAD_CHANNELS)], kvw.at[own, 1])
    load("q", q_in.at[:, part(side, wide)], qw.at[side])
    load("q", do_in.at[:, part(side, wide)], dow.at[side])

    @pl.when(jnp.logical_not(has_before))
    def _():
        for h in range(2):
            docs[h] = jnp.full(docs.shape[1:], -1, jnp.int32)
            kvw[h] = jnp.zeros(kvw.shape[1:], BF16)

    @pl.when(jnp.logical_not(has_after))
    def _():
        docs[4] = jnp.full(docs.shape[1:], -1, jnp.int32)
        gr[...] = jnp.zeros(gr.shape, BF16)

    @pl.when(jnp.logical_not(has_outer))
    def _():
        zbuf[...] = jnp.zeros(zbuf.shape, BF16)

    @pl.when(jnp.logical_not(is_first | has_before))
    def _():
        lbuf[last] = jnp.zeros(lbuf.shape[1:], BF16)

    def announce():
        greeted = (has_before & jnp.logical_not(at_front)).astype(jnp.int32) + has_after.astype(jnp.int32)
        pl.semaphore_wait(barrier, 1 + 2 * greeted)
        tell(ready, after, at_back)
        start([docs_mate])
        start(docs_after + kv_after, has_after)
        start(docs_before, has_before & is_first & jnp.logical_not(at_front))
        start([kv_mate, q_mate, do_mate])

    sends_early = lax.rem(me, ROUND) >= ROUND // 2
    drained("local", [("doc", docs.at[own]), ("kv", kvo)])

    @pl.when(sends_early)
    def _():
        announce()

    rows_i = lax.broadcasted_iota(jnp.int32, square, 0)
    cols_i = lax.broadcasted_iota(jnp.int32, square, 1)
    triu = (rows_i <= cols_i).astype(F32).astype(BF16)
    drained("local", [("ld", ldb)])
    sums = dot(bf16_parts(ldb[...], 3), triu)
    lam_t = (sums[2 * heads :] + sums[heads : 2 * heads]) + sums[:heads]
    for c in range(CHUNKS):
        lt[c] = lam_t[c * chunk_heads : (c + 1) * chunk_heads]
    exits = jnp.exp(lam_t[:, tokens - 1 : tokens] - lam_t)
    entries = jnp.exp(lam_t)
    for c in range(CHUNKS):
        wrow[0, c] = exits[c * chunk_heads : (c + 1) * chunk_heads]
        wrow[1, c] = entries[c * chunk_heads : (c + 1) * chunk_heads]

    doc_row = docs[own].astype(F32)
    doc_first = doc_row[:, 0:1]
    doc_last = doc_row[:, tokens - 1 : tokens]
    doc_rows = jnp.broadcast_to(doc_row, square)
    doc_cols = doc_rows.T
    drained("local", [("states", srw)])
    writes = srw[0]
    reads = srw[1]
    writes_in = jnp.where(doc_cols == doc_last, writes.astype(F32), 0.0)
    reads_in = jnp.where(doc_cols == doc_first, reads.astype(F32), 0.0)
    srw[0] = writes_in.astype(BF16)
    srw[1] = reads_in.astype(BF16)
    srwt[0] = writes_in.T
    srwt[1] = reads_in.T

    lane = lax.broadcasted_iota(jnp.int32, (1, 2 * half), 1)
    low_half = (lane < half).astype(F32).astype(BF16)
    high_half = (lane >= half).astype(F32).astype(BF16)

    def two_heads(tile):
        return jnp.concatenate([tile * low_half, tile * high_half], axis=0)

    def state(d, c):
        weights = wrow[d, c]
        for j in range(chunk_heads // 2):
            cols = slice(2 * j * half, (2 * j + 2) * half)
            left_side = [(srwt[d] * weights[h : h + 1]).astype(BF16) for h in (2 * j, 2 * j + 1)]
            st[d, c, :, cols] = dot(jnp.concatenate(left_side, axis=1), two_heads(xc[d, c, :, cols])).astype(BF16)

    drained("local", [("x", xc)])

    def first_state(c):
        state(side, c)
        start([mate_send(c)], sends_early)

    over(CHUNKS, first_state)

    @pl.when(jnp.logical_not(sends_early))
    def _():
        announce()
        over(CHUNKS, lambda c: mate_send(c).start())

    over(CHUNKS, lambda c: state(other, c))

    whole = (doc_first == doc_last).astype(F32)

    def gains(c):
        ends = wrow[1, c][:, tokens - 1 : tokens] * whole
        pairs = [
            jnp.where(lane < half, ends[h : h + 1], ends[h + 1 : h + 2]) for h in range(0, chunk_heads, 2)
        ]
        gain[c] = jnp.concatenate(pairs, axis=1)

    over(CHUNKS, gains)
    start([gain_send])

    def edge(early, late):
        ends = docs[early].astype(F32)[:, tokens - 1 : tokens]
        return (docs[late].astype(F32)[:, 0:1] == ends).astype(F32)

    drained("recv", [("docs_mate", docs.at[own])])
    joined = edge(2, 3)

    def combine(c):
        drain("recv", "mate", mbuf.at[c], c)
        cz[c] = (st[other, c].astype(F32) + (gain[c] * joined) * mbuf[c].astype(F32)).astype(BF16)
        start([outer_send(c)], has_outer & (is_first | (c < last)))

    @pl.when(at_front & is_first)
    def _():
        pl.semaphore_wait(ready, 2)
        start(docs_before)

    over(CHUNKS, combine)
    start([low_send, far_send, high_send], has_outer & jnp.logical_not(is_first))

    scale[0] = bf16_parts(exits, 2).T
    scale[1] = bf16_parts(entries, 2).T
    spread_at = lax.broadcasted_iota(jnp.int32, (2 * heads, chunk_cols), 0)
    spread_head = lax.broadcasted_iota(jnp.int32, (2 * heads, chunk_cols), 1) // half

    same = doc_rows == doc_cols
    gmask[0] = jnp.where(same & (rows_i >= cols_i), dot(reads, writes, ((1,), (1,))), 0.0)
    gmask[1] = jnp.where(same & (cols_i >= rows_i), dot(writes, reads, ((1,), (1,))), 0.0)

    def inside_block(c):
        head = spread_head + c * chunk_heads
        hot = ((spread_at == head) | (spread_at == head + heads)).astype(F32).astype(BF16)
        for d in range(2):
            sc[d, c] = dot(scale[d], hot)
        for j in range(chunk_heads // 2):
            fwd = []
            bwd = []
            for h in (2 * j, 2 * j + 1):
                lam_rows = jnp.broadcast_to(lt[c, h : h + 1, :], square)
                decay = jnp.exp(-jnp.abs(lam_rows.T - lam_rows))
                fwd.append((decay * gmask[0]).astype(BF16))
                bwd.append((decay * gmask[1]).astype(BF16))
            cols = slice(2 * j * half, (2 * j + 2) * half)
            for d, weights in ((0, fwd), (1, bwd)):
                local[d, c, :, cols] = dot(jnp.concatenate(weights, axis=1), two_heads(xc[d, c, :, cols]))

    over(CHUNKS, inside_block)

    @pl.when(at_front & jnp.logical_not(is_first))
    def _():
        pl.semaphore_wait(ready, 2)

    drained("local", [("own_kv", kvw.at[own]), ("q", qw)])
    drained("recv", [("q_mate", qw), ("kv_mate", kvw.at[own])])
    drained("recv", [("docs_after", docs.at[0:2]), ("kv_after", kvw.at[0:2])], has_before)
    gacc[...] = jnp.zeros(gacc.shape, F32)

    def attend(pos):
        rows = jnp.broadcast_to(docs[2 + pos].astype(F32), square)
        for n in range(3):
            keep = jnp.broadcast_to(docs[pos + n].astype(F32), square).T == rows
            if n == 2:
                keep = keep & (cols_i >= rows_i)
            bias[n * tokens : (n + 1) * tokens] = jnp.where(keep, 0.0, -1e30)

        def two_queries(pair):
            def pair_of(ref):
                return jnp.concatenate(
                    [ref[pos, :, pl.ds(pl.multiple_of((2 * pair + i) * HEAD_CHANNELS, HEAD_CHANNELS), HEAD_CHANNELS)] for i in range(2)],
                    axis=0,
                )

            keys = jnp.concatenate([kvw[pos + n, 0] for n in range(3)], axis=0)
            values = jnp.concatenate([kvw[pos + n, 1] for n in range(3)], axis=0)
            mask = jnp.concatenate([bias[...], bias[...]], axis=1)
            raw = dot(keys, pair_of(qw), ((1,), (1,))) + mask
            peak = jnp.max(raw, axis=0, keepdims=True)
            raised = jnp.exp((raw - peak) * inv_root)
            probs = (raised * (1.0 / jnp.sum(raised, axis=0, keepdims=True))).astype(BF16)
            pt[pair] = probs
            out_t = dot(values.T, probs)
            for i in range(2):
                cols = pl.ds(pl.multiple_of((2 * pair + i) * HEAD_CHANNELS, HEAD_CHANNELS), HEAD_CHANNELS)
                aob[pos, :, cols] = out_t[:, i * tokens : (i + 1) * tokens].T.astype(BF16)
            prob_grad = dot(values, pair_of(dow), ((1,), (1,)))
            single = probs.astype(F32)
            inner = jnp.sum(single * prob_grad, axis=0, keepdims=True)
            dst[pair] = (single * (prob_grad - inner) * inv_root).astype(BF16)

        over(per_group // 2, two_queries)
        for n, (probs_ref, rows_ref) in enumerate(((dst, qw), (pt, dow))):
            grad = dot(
                jnp.concatenate([probs_ref[pair] for pair in range(per_group // 2)], axis=1),
                jnp.concatenate(
                    [rows_ref[pos, :, i * HEAD_CHANNELS : (i + 1) * HEAD_CHANNELS] for i in range(per_group)], axis=0
                ),
            )
            for m in range(3):
                gacc[pos + m, n] += grad[m * tokens : (m + 1) * tokens]
            gs[pos, n] = gacc[pos, n].astype(BF16)
        start([grads_before(pos)], has_before)

    over(2, attend)
    start([ao_mate])
    for n in range(2):
        gsm[n] = gacc[2 + other, n].astype(BF16)
    start([grads_mate])
    ao[side] = aob[side]

    drained("recv", [("docs_before", docs.at[4])], has_after)
    in_before = edge(1, 2)
    in_after = edge(3, 4)
    outer_joined = jnp.where(is_first, in_before, in_after)
    mate_joined = jnp.where(is_first, in_after, in_before)

    def finish(d, c, rows, carried):
        mix[d, :, part(c, chunk_cols)] = (local[d, c] + sc[1 - d, c] * dot(rows, carried)).astype(BF16)

    rows = (srw[other].astype(F32) * outer_joined).astype(BF16)

    def from_outside(c):
        drained("recv", [("outer", zbuf.at[c], c)], has_outer)
        relay_send(c).start()
        finish(side, c, rows, zbuf[c])

    over(last, from_outside)

    @pl.when(is_first)
    def _():
        drained("recv", [("low", zbuf.at[last, :, halves[0]])], has_outer)
        low_relay.start()
        drained("recv", [("high", zbuf.at[last, :, halves[1]])], has_outer)

    @pl.when(jnp.logical_not(is_first))
    def _():
        drained("recv", [("outer", zbuf.at[last], last)], has_outer)
        relay_send(last).start()

    finish(side, last, rows, zbuf[last])
    mate_rows = (srw[side].astype(F32) * joined).astype(BF16)
    drained("recv", [("gain", gain)])

    def carry_from_mate(c):
        carried = mbuf[c].astype(F32) + (gmate[c] * mate_joined) * lbuf[c].astype(F32)
        finish(other, c, mate_rows, carried.astype(BF16))

    def from_mate(c):
        drain("recv", "relay", lbuf.at[c], c)
        carry_from_mate(c)

    sent = [("docs_mate", docs.at[own]), ("kv_mate", kvo.at[0]), ("q_mate", qw), ("gain", gain), ("mate", mbuf)]
    drained("send", sent)
    drained("send", [("docs_after", docs.at[0:2]), ("kv_after", kvo)], has_after)
    drained("send", [("docs_before", docs.at[0:2])], has_before & is_first)
    drained("send", [("outer", cz)], has_outer & is_first)
    low_part, high_part = (cz.at[last, :, cols] for cols in halves)
    drained(
        "send",
        [("outer", cz.at[0:last]), ("low", low_part), ("high", high_part), ("far", high_part)],
        has_outer & jnp.logical_not(is_first),
    )
    over(last, from_mate)

    @pl.when(is_first)
    def _():
        drained("recv", [("relay", lbuf.at[last], last)])

    @pl.when(jnp.logical_not(is_first))
    def _():
        drained("recv", [("low_relay", lbuf.at[last, :, halves[0]])])
        drained("recv", [("far", lbuf.at[last, :, halves[1]])], has_before)

    carry_from_mate(last)

    drained("recv", [("ao", aom), ("grads_mate", grm)])
    ao[other] = aom[...]
    drained("recv", [("grads", gr)], has_after)
    for n in range(2):
        gkv[side, n] = (gacc[own, n] + gr[side, n].astype(F32)).astype(BF16)
        gkv[other, n] = (grm[n].astype(F32) + gr[other, n].astype(F32)).astype(BF16)

    drained("send", [("ao", aom), ("grads_mate", gsm)])
    drained("send", [("grads", gs)], has_before)
    drained("send", [("relay", zbuf.at[0:last]), ("low_relay", low_part)], is_first)
    drained("send", [("relay", zbuf)], jnp.logical_not(is_first))


def store_kernel(ao, mix, gkv, ao_out, mo_out, gk_out, gv_out, gx_out, sem):
    moves = [(mix.at[0], mo_out), (mix.at[1], gx_out)]
    for h in range(2):
        wide = ao.shape[2]
        moves.append((ao.at[h], ao_out.at[:, pl.ds(h * wide, wide)]))
        for n, out in enumerate((gk_out, gv_out)):
            moves.append((gkv.at[h, n], out.at[:, pl.ds(h * HEAD_CHANNELS, HEAD_CHANNELS)]))
    copies = [pltpu.make_async_copy(src, dst, sem.at[n]) for n, (src, dst) in enumerate(moves)]
    for copy in copies:
        copy.start()
    for copy in copies:
        copy.wait()


def shards(q, k, v, x, ld, sw, sr, doc, do, cm):
    tokens = q.shape[0]
    assert k.shape[1] == 2 * HEAD_CHANNELS
    wide = q.shape[1] // 2
    heads = ld.shape[1]
    states = sw.shape[1]
    chunk_cols = x.shape[1] // CHUNKS
    span = 3 * tokens
    square = (tokens, HEAD_CHANNELS)
    vmem = pltpu.VMEM
    hbm = pl.BlockSpec(memory_space=pltpu.HBM)
    onchip = pl.BlockSpec(memory_space=pltpu.VMEM)
    shape = jax.ShapeDtypeStruct
    operands = [
        pltpu.with_memory_space_constraint(a, pltpu.HBM) for a in (q, k, v, x, ld.T, sw, sr, doc.reshape(1, tokens), do, cm)
    ]
    parts = pl.pallas_call(
        step_kernel,
        out_shape=(shape((2, tokens, wide), BF16), shape((2,) + x.shape, BF16), shape((2, 2) + square, BF16)),
        in_specs=[hbm] * 10,
        out_specs=[onchip] * 3,
        scratch_shapes=[
            vmem((2, tokens, wide), BF16),
            vmem((2, tokens, wide), BF16),
            vmem((2, CHUNKS, tokens, chunk_cols), BF16),
            vmem((heads, tokens), F32),
            vmem((2, tokens, states), BF16),
            vmem((2, states, tokens), F32),
            vmem((5, 1, tokens), jnp.int32),
            vmem((2, 2) + square, BF16),
            vmem((4, 2) + square, BF16),
            vmem((2, tokens, 2 * heads), BF16),
            vmem((2, CHUNKS, heads // CHUNKS, tokens), F32),
            vmem((2, CHUNKS, tokens, chunk_cols), F32),
            vmem((CHUNKS, heads // CHUNKS, tokens), F32),
            vmem((2, CHUNKS, states, chunk_cols), BF16),
            vmem((CHUNKS, states, chunk_cols), BF16),
            vmem((CHUNKS, states, chunk_cols), BF16),
            vmem((CHUNKS, states, chunk_cols), BF16),
            vmem((CHUNKS, states, chunk_cols), BF16),
            vmem((CHUNKS, 1, chunk_cols), F32),
            vmem((CHUNKS, 1, chunk_cols), F32),
            vmem((2, CHUNKS, tokens, chunk_cols), F32),
            vmem((wide // HEAD_CHANNELS // 2, span, 2 * tokens), BF16),
            vmem((wide // HEAD_CHANNELS // 2, span, 2 * tokens), BF16),
            vmem((span, tokens), F32),
            vmem((2, tokens, wide), BF16),
            vmem((tokens, wide), BF16),
            vmem((2, 2) + square, BF16),
            vmem((4, 2) + square, F32),
            vmem((2, 2) + square, BF16),
            vmem((2,) + square, BF16),
            vmem((2,) + square, BF16),
            vmem((2, tokens, tokens), F32),
            pltpu.SemaphoreType.DMA((7,)),
            pltpu.SemaphoreType.DMA((17,)),
            pltpu.SemaphoreType.DMA((14 + 3 * CHUNKS,)),
            pltpu.SemaphoreType.REGULAR,
        ],
        compiler_params=pltpu.CompilerParams(collective_id=0, has_side_effects=True, vmem_limit_bytes=40 << 20),
        name="step",
    )(*operands)
    return pl.pallas_call(
        store_kernel,
        out_shape=(
            shape(q.shape, BF16), shape(x.shape, BF16), shape(k.shape, BF16), shape(v.shape, BF16), shape(x.shape, BF16),
        ),
        in_specs=[onchip] * 3,
        out_specs=[hbm] * 5,
        scratch_shapes=[pltpu.SemaphoreType.DMA((8,))],
        compiler_params=pltpu.CompilerParams(vmem_limit_bytes=8 << 20),
        name="store",
    )(*parts)


def solution(mesh):
    both = P("ctx", "tp")
    return jax.shard_map(
        shards,
        mesh=mesh,
        in_specs=(both, both, both, both, both, P("ctx", None), P("ctx", None), P("ctx"), both, both),
        out_specs=(both,) * 5,
        check_vma=False,
    )
```

```python
import math

import jax
import jax.numpy as jnp
from jax import lax
from jax.experimental import pallas as pl
from jax.experimental.pallas import tpu as pltpu
from jax.sharding import PartitionSpec as P

HEAD_CHANNELS = 128
CHUNKS = 4
DOUBLED = 256
ROUND = 16
MESH = pl.DeviceIdType.MESH
F32 = jnp.float32
BF16 = jnp.bfloat16


def dot(a, b, contract=((1,), (0,))):
    return lax.dot_general(a, b, (contract, ((), ())), preferred_element_type=F32)


def bf16_parts(values, count):
    parts = []
    for _ in range(count):
        parts.append(values.astype(BF16))
        values = values - parts[-1].astype(F32)
    return jnp.concatenate(parts, axis=0)


def step_kernel(
    q_in, k_in, v_in, x_in, ld_in, sw_in, sr_in, doc_in, do_in, cm_in,
    ao, mix, gkv,
    qw, dow, xc, ldb, srw, srwt, docs, kvo, kvw, scale, wrow, sc, lt, st, mbuf, cz, zbuf, lbuf, gain, gmate,
    local, pt, dst, bias, aob, aom, gs, gacc, gr, gsm, grm, gmask, lsem, ssem, rsem, ready,
):
    tokens = qw.shape[1]
    wide = qw.shape[2]
    heads = ld_in.shape[0]
    per_group = wide // HEAD_CHANNELS
    chunk_cols = x_in.shape[1] // CHUNKS
    chunk_heads = heads // CHUNKS
    half = chunk_cols // chunk_heads
    inv_root = 1.0 / math.sqrt(HEAD_CHANNELS)
    square = (tokens, tokens)

    count = lax.axis_size("ctx")
    me = lax.axis_index("ctx")
    row = lax.axis_index("tp")
    side = lax.rem(me, 2)
    other = 1 - side
    own = 2 + side
    mate = me + 1 - 2 * side
    outer = me - 1 + 2 * side
    before = [me - side - 2, me - side - 1]
    after = [me - side + 2, me - side + 3]
    has_before = me >= 2
    has_after = me < count - 2
    is_first = side == 0
    at_front = has_before & (lax.rem(me, ROUND) < 2)
    at_back = has_after & (lax.rem(me, ROUND) >= ROUND - 2)
    has_outer = (is_first & has_before) | (jnp.logical_not(is_first) & has_after)

    sems = {}

    def sem(kind, name, width=1):
        ref, used = {"local": (lsem, 0), "send": (ssem, 1), "recv": (rsem, 2)}[kind]
        if (kind, name) not in sems:
            sems[kind, name] = sems.get(used, 0)
            sems[used] = sems.get(used, 0) + width
        return ref, sems[kind, name]

    def drain(kind, name, ref, at=0):
        array, first = sem(kind, name)
        pltpu.make_async_copy(ref, ref, array.at[first + at]).wait()

    def load(name, src, dst_ref):
        array, first = sem("local", name)
        pltpu.make_async_copy(src, dst_ref, array.at[first]).start()

    def send(name, src, dst_ref, target, at=0, width=1):
        out, out_first = sem("send", name)
        into, into_first = sem("recv", name, width)
        return pltpu.make_async_remote_copy(
            src_ref=src, dst_ref=dst_ref, send_sem=out.at[out_first], recv_sem=into.at[into_first + at],
            device_id=(target, row), device_id_type=MESH,
        )

    def each(copies, act, there):
        if there is None:
            for copy in copies:
                act(copy)
        else:
            @pl.when(there)
            def _():
                for copy in copies:
                    act(copy)

    def start(copies, there=None):
        each(copies, lambda copy: copy.start(), there)

    def drained(kind, waits, there=None):
        each(waits, lambda wait: drain(kind, *wait), there)

    def over(count, body):
        lax.fori_loop(0, count, lambda c, carry: (body(c), carry)[1], 0)

    def part(which, width):
        return pl.ds(pl.multiple_of(which * width, width), width)

    docs_mate = send("docs_mate", docs.at[own], docs.at[own], mate)
    docs_after = [send("docs_after", docs.at[own], docs.at[side], after[h]) for h in range(2)]
    docs_before = [send("docs_before", docs.at[2], docs.at[4], before[h]) for h in range(2)]
    kv_mate = send("kv_mate", kvo.at[other], kvw.at[own], mate)
    kv_after = [send("kv_after", kvo.at[h], kvw.at[side], after[h]) for h in range(2)]
    q_mate = send("q_mate", q_in.at[:, part(other, wide)], qw.at[side], mate)
    do_mate = send("q_mate", do_in.at[:, part(other, wide)], dow.at[side], mate)
    gain_send = send("gain", gain, gmate, mate)
    ao_mate = send("ao", aob.at[other], aom, mate)
    grads_mate = send("grads_mate", gsm, grm, mate)
    sem("recv", "mate", CHUNKS)
    sem("recv", "outer", CHUNKS)
    sem("recv", "relay", CHUNKS)

    def grads_before(h):
        return send("grads", gs.at[h], gr.at[side], before[0] + h)

    def mate_send(c):
        return send("mate", st.at[side, c], mbuf.at[c], mate, c)

    def outer_send(c):
        return send("outer", cz.at[c], zbuf.at[c], outer, c)

    def relay_send(c):
        return send("relay", zbuf.at[c], lbuf.at[c], mate, c)

    last = CHUNKS - 1
    halves = [pl.ds(0, chunk_cols - DOUBLED), pl.ds(chunk_cols - DOUBLED, DOUBLED)]
    low_send = send("low", cz.at[last, :, halves[0]], zbuf.at[last, :, halves[0]], outer)
    high_send = send("high", cz.at[last, :, halves[1]], zbuf.at[last, :, halves[1]], outer)
    far_send = send("far", cz.at[last, :, halves[1]], lbuf.at[last, :, halves[1]], outer - 1 + 2 * side)
    low_relay = send("low_relay", zbuf.at[last, :, halves[0]], lbuf.at[last, :, halves[0]], mate)

    barrier = pltpu.get_barrier_semaphore()

    def tell(semaphore, targets, there=None):
        each(
            targets,
            lambda target: pl.semaphore_signal(semaphore, inc=1, device_id=(target, row), device_id_type=MESH),
            there,
        )

    tell(barrier, [mate])
    tell(barrier, before, has_before)
    tell(barrier, after, has_after & jnp.logical_not(at_back))

    load("doc", doc_in, docs.at[own])
    for h in range(2):
        cols = pl.ds(h * HEAD_CHANNELS, HEAD_CHANNELS)
        load("kv", k_in.at[:, cols], kvo.at[h, 0])
        load("kv", v_in.at[:, cols], kvo.at[h, 1])
    load("ld", ld_in, ldb)
    load("states", sw_in, srw.at[0])
    load("states", sr_in, srw.at[1])
    for d, src in enumerate((x_in, cm_in)):
        for c in range(CHUNKS):
            load("x", src.at[:, pl.ds(c * chunk_cols, chunk_cols)], xc.at[d, c])
    load("own_kv", k_in.at[:, part(side, HEAD_CHANNELS)], kvw.at[own, 0])
    load("own_kv", v_in.at[:, part(side, HEAD_CHANNELS)], kvw.at[own, 1])
    load("q", q_in.at[:, part(side, wide)], qw.at[side])
    load("q", do_in.at[:, part(side, wide)], dow.at[side])

    @pl.when(jnp.logical_not(has_before))
    def _():
        for h in range(2):
            docs[h] = jnp.full(docs.shape[1:], -1, jnp.int32)
            kvw[h] = jnp.zeros(kvw.shape[1:], BF16)

    @pl.when(jnp.logical_not(has_after))
    def _():
        docs[4] = jnp.full(docs.shape[1:], -1, jnp.int32)
        gr[...] = jnp.zeros(gr.shape, BF16)

    @pl.when(jnp.logical_not(has_outer))
    def _():
        zbuf[...] = jnp.zeros(zbuf.shape, BF16)

    @pl.when(jnp.logical_not(is_first | has_before))
    def _():
        lbuf[last] = jnp.zeros(lbuf.shape[1:], BF16)

    def announce():
        greeted = (has_before & jnp.logical_not(at_front)).astype(jnp.int32) + has_after.astype(jnp.int32)
        pl.semaphore_wait(barrier, 1 + 2 * greeted)
        tell(ready, after, at_back)
        start([docs_mate])
        start(docs_after + kv_after, has_after)
        start(docs_before, has_before & is_first & jnp.logical_not(at_front))
        start([kv_mate, q_mate, do_mate])

    sends_early = lax.rem(me, ROUND) >= ROUND // 2
    drained("local", [("doc", docs.at[own]), ("kv", kvo)])

    @pl.when(sends_early)
    def _():
        announce()

    rows_i = lax.broadcasted_iota(jnp.int32, square, 0)
    cols_i = lax.broadcasted_iota(jnp.int32, square, 1)
    triu = (rows_i <= cols_i).astype(F32).astype(BF16)
    drained("local", [("ld", ldb)])
    sums = dot(bf16_parts(ldb[...], 3), triu)
    lam_t = (sums[2 * heads :] + sums[heads : 2 * heads]) + sums[:heads]
    for c in range(CHUNKS):
        lt[c] = lam_t[c * chunk_heads : (c + 1) * chunk_heads]
    exits = jnp.exp(lam_t[:, tokens - 1 : tokens] - lam_t)
    entries = jnp.exp(lam_t)
    for c in range(CHUNKS):
        wrow[0, c] = exits[c * chunk_heads : (c + 1) * chunk_heads]
        wrow[1, c] = entries[c * chunk_heads : (c + 1) * chunk_heads]

    doc_row = docs[own].astype(F32)
    doc_first = doc_row[:, 0:1]
    doc_last = doc_row[:, tokens - 1 : tokens]
    doc_rows = jnp.broadcast_to(doc_row, square)
    doc_cols = doc_rows.T
    drained("local", [("states", srw)])
    writes = srw[0]
    reads = srw[1]
    writes_in = jnp.where(doc_cols == doc_last, writes.astype(F32), 0.0)
    reads_in = jnp.where(doc_cols == doc_first, reads.astype(F32), 0.0)
    srw[0] = writes_in.astype(BF16)
    srw[1] = reads_in.astype(BF16)
    srwt[0] = writes_in.T
    srwt[1] = reads_in.T

    lane = lax.broadcasted_iota(jnp.int32, (1, 2 * half), 1)
    low_half = (lane < half).astype(F32).astype(BF16)
    high_half = (lane >= half).astype(F32).astype(BF16)

    def two_heads(tile):
        return jnp.concatenate([tile * low_half, tile * high_half], axis=0)

    def state(d, c):
        weights = wrow[d, c]
        for j in range(chunk_heads // 2):
            cols = slice(2 * j * half, (2 * j + 2) * half)
            left_side = [(srwt[d] * weights[h : h + 1]).astype(BF16) for h in (2 * j, 2 * j + 1)]
            st[d, c, :, cols] = dot(jnp.concatenate(left_side, axis=1), two_heads(xc[d, c, :, cols])).astype(BF16)

    drained("local", [("x", xc)])

    def first_state(c):
        state(side, c)
        start([mate_send(c)], sends_early)

    over(CHUNKS, first_state)

    @pl.when(jnp.logical_not(sends_early))
    def _():
        announce()
        over(CHUNKS, lambda c: mate_send(c).start())

    over(CHUNKS, lambda c: state(other, c))

    whole = (doc_first == doc_last).astype(F32)

    def gains(c):
        ends = wrow[1, c][:, tokens - 1 : tokens] * whole
        pairs = [
            jnp.where(lane < half, ends[h : h + 1], ends[h + 1 : h + 2]) for h in range(0, chunk_heads, 2)
        ]
        gain[c] = jnp.concatenate(pairs, axis=1)

    over(CHUNKS, gains)
    start([gain_send])

    def edge(early, late):
        ends = docs[early].astype(F32)[:, tokens - 1 : tokens]
        return (docs[late].astype(F32)[:, 0:1] == ends).astype(F32)

    drained("recv", [("docs_mate", docs.at[own])])
    joined = edge(2, 3)

    def combine(c):
        drain("recv", "mate", mbuf.at[c], c)
        cz[c] = (st[other, c].astype(F32) + (gain[c] * joined) * mbuf[c].astype(F32)).astype(BF16)
        start([outer_send(c)], has_outer & (is_first | (c < last)))

    @pl.when(at_front & is_first)
    def _():
        pl.semaphore_wait(ready, 2)
        start(docs_before)

    over(CHUNKS, combine)
    start([low_send, far_send, high_send], has_outer & jnp.logical_not(is_first))

    scale[0] = bf16_parts(exits, 2).T
    scale[1] = bf16_parts(entries, 2).T
    spread_at = lax.broadcasted_iota(jnp.int32, (2 * heads, chunk_cols), 0)
    spread_head = lax.broadcasted_iota(jnp.int32, (2 * heads, chunk_cols), 1) // half

    same = doc_rows == doc_cols
    gmask[0] = jnp.where(same & (rows_i >= cols_i), dot(reads, writes, ((1,), (1,))), 0.0)
    gmask[1] = jnp.where(same & (cols_i >= rows_i), dot(writes, reads, ((1,), (1,))), 0.0)

    def inside_block(c):
        head = spread_head + c * chunk_heads
        hot = ((spread_at == head) | (spread_at == head + heads)).astype(F32).astype(BF16)
        for d in range(2):
            sc[d, c] = dot(scale[d], hot)
        for j in range(chunk_heads // 2):
            fwd = []
            bwd = []
            for h in (2 * j, 2 * j + 1):
                lam_rows = jnp.broadcast_to(lt[c, h : h + 1, :], square)
                decay = jnp.exp(-jnp.abs(lam_rows.T - lam_rows))
                fwd.append((decay * gmask[0]).astype(BF16))
                bwd.append((decay * gmask[1]).astype(BF16))
            cols = slice(2 * j * half, (2 * j + 2) * half)
            for d, weights in ((0, fwd), (1, bwd)):
                local[d, c, :, cols] = dot(jnp.concatenate(weights, axis=1), two_heads(xc[d, c, :, cols]))

    over(CHUNKS, inside_block)

    @pl.when(at_front & jnp.logical_not(is_first))
    def _():
        pl.semaphore_wait(ready, 2)

    drained("local", [("own_kv", kvw.at[own]), ("q", qw)])
    drained("recv", [("q_mate", qw), ("kv_mate", kvw.at[own])])
    drained("recv", [("docs_after", docs.at[0:2]), ("kv_after", kvw.at[0:2])], has_before)
    gacc[...] = jnp.zeros(gacc.shape, F32)

    def attend(pos):
        rows = jnp.broadcast_to(docs[2 + pos].astype(F32), square)
        for n in range(3):
            keep = jnp.broadcast_to(docs[pos + n].astype(F32), square).T == rows
            if n == 2:
                keep = keep & (cols_i >= rows_i)
            bias[n * tokens : (n + 1) * tokens] = jnp.where(keep, 0.0, -1e30)

        def two_queries(pair):
            def pair_of(ref):
                return jnp.concatenate(
                    [ref[pos, :, pl.ds(pl.multiple_of((2 * pair + i) * HEAD_CHANNELS, HEAD_CHANNELS), HEAD_CHANNELS)] for i in range(2)],
                    axis=0,
                )

            keys = jnp.concatenate([kvw[pos + n, 0] for n in range(3)], axis=0)
            values = jnp.concatenate([kvw[pos + n, 1] for n in range(3)], axis=0)
            mask = jnp.concatenate([bias[...], bias[...]], axis=1)
            raw = dot(keys, pair_of(qw), ((1,), (1,))) + mask
            peak = jnp.max(raw, axis=0, keepdims=True)
            raised = jnp.exp((raw - peak) * inv_root)
            probs = (raised * (1.0 / jnp.sum(raised, axis=0, keepdims=True))).astype(BF16)
            pt[pair] = probs
            out_t = dot(values.T, probs)
            for i in range(2):
                cols = pl.ds(pl.multiple_of((2 * pair + i) * HEAD_CHANNELS, HEAD_CHANNELS), HEAD_CHANNELS)
                aob[pos, :, cols] = out_t[:, i * tokens : (i + 1) * tokens].T.astype(BF16)
            prob_grad = dot(values, pair_of(dow), ((1,), (1,)))
            single = probs.astype(F32)
            inner = jnp.sum(single * prob_grad, axis=0, keepdims=True)
            dst[pair] = (single * (prob_grad - inner) * inv_root).astype(BF16)

        over(per_group // 2, two_queries)
        for n, (probs_ref, rows_ref) in enumerate(((dst, qw), (pt, dow))):
            grad = dot(
                jnp.concatenate([probs_ref[pair] for pair in range(per_group // 2)], axis=1),
                jnp.concatenate(
                    [rows_ref[pos, :, i * HEAD_CHANNELS : (i + 1) * HEAD_CHANNELS] for i in range(per_group)], axis=0
                ),
            )
            for m in range(3):
                gacc[pos + m, n] += grad[m * tokens : (m + 1) * tokens]
            gs[pos, n] = gacc[pos, n].astype(BF16)
        start([grads_before(pos)], has_before)

    over(2, attend)
    start([ao_mate])
    for n in range(2):
        gsm[n] = gacc[2 + other, n].astype(BF16)
    start([grads_mate])
    ao[side] = aob[side]

    drained("recv", [("docs_before", docs.at[4])], has_after)
    in_before = edge(1, 2)
    in_after = edge(3, 4)
    outer_joined = jnp.where(is_first, in_before, in_after)
    mate_joined = jnp.where(is_first, in_after, in_before)

    def finish(d, c, rows, carried):
        mix[d, :, part(c, chunk_cols)] = (local[d, c] + sc[1 - d, c] * dot(rows, carried)).astype(BF16)

    rows = (srw[other].astype(F32) * outer_joined).astype(BF16)

    mate_rows = (srw[side].astype(F32) * joined).astype(BF16)

    def carry_from_mate(c):
        carried = mbuf[c].astype(F32) + (gmate[c] * mate_joined) * lbuf[c].astype(F32)
        finish(other, c, mate_rows, carried.astype(BF16))

    def from_mate(c):
        drain("recv", "relay", lbuf.at[c], c)
        carry_from_mate(c)

    def carries_from_mate():
        drained("recv", [("gain", gain)])
        over(last, from_mate)

        @pl.when(is_first)
        def _():
            drained("recv", [("relay", lbuf.at[last], last)])

        @pl.when(jnp.logical_not(is_first))
        def _():
            drained("recv", [("low_relay", lbuf.at[last, :, halves[0]])])
            drained("recv", [("far", lbuf.at[last, :, halves[1]])], has_before)

        carry_from_mate(last)

    def gradients():
        drained("recv", [("ao", aom), ("grads_mate", grm)])
        ao[other] = aom[...]
        drained("recv", [("grads", gr)], has_after)
        for n in range(2):
            gkv[side, n] = (gacc[own, n] + gr[side, n].astype(F32)).astype(BF16)
            gkv[other, n] = (grm[n].astype(F32) + gr[other, n].astype(F32)).astype(BF16)

    def from_outside(c):
        drained("recv", [("outer", zbuf.at[c], c)], has_outer)
        relay_send(c).start()
        finish(side, c, rows, zbuf[c])

    over(last, from_outside)

    @pl.when(is_first)
    def _():
        drained("recv", [("low", zbuf.at[last, :, halves[0]])], has_outer)
        low_relay.start()

        @pl.when(at_front)
        def _():
            carries_from_mate()

        drained("recv", [("high", zbuf.at[last, :, halves[1]])], has_outer)

    @pl.when(jnp.logical_not(is_first))
    def _():
        drained("recv", [("outer", zbuf.at[last], last)], has_outer)
        relay_send(last).start()

    finish(side, last, rows, zbuf[last])
    sent = [("docs_mate", docs.at[own]), ("kv_mate", kvo.at[0]), ("q_mate", qw), ("gain", gain), ("mate", mbuf)]
    drained("send", sent)
    drained("send", [("docs_after", docs.at[0:2]), ("kv_after", kvo)], has_after)
    drained("send", [("docs_before", docs.at[0:2])], has_before & is_first)
    drained("send", [("outer", cz)], has_outer & is_first)
    low_part, high_part = (cz.at[last, :, cols] for cols in halves)
    drained(
        "send",
        [("outer", cz.at[0:last]), ("low", low_part), ("high", high_part), ("far", high_part)],
        has_outer & jnp.logical_not(is_first),
    )

    @pl.when(jnp.logical_not(at_front & is_first))
    def _():
        carries_from_mate()

    gradients()
    drained("send", [("ao", aom), ("grads_mate", gsm)])
    drained("send", [("grads", gs)], has_before)
    drained("send", [("relay", zbuf.at[0:last]), ("low_relay", low_part)], is_first)
    drained("send", [("relay", zbuf)], jnp.logical_not(is_first))


def store_kernel(ao, mix, gkv, ao_out, mo_out, gk_out, gv_out, gx_out, sem):
    moves = [(mix.at[0], mo_out), (mix.at[1], gx_out)]
    for h in range(2):
        wide = ao.shape[2]
        moves.append((ao.at[h], ao_out.at[:, pl.ds(h * wide, wide)]))
        for n, out in enumerate((gk_out, gv_out)):
            moves.append((gkv.at[h, n], out.at[:, pl.ds(h * HEAD_CHANNELS, HEAD_CHANNELS)]))
    copies = [pltpu.make_async_copy(src, dst, sem.at[n]) for n, (src, dst) in enumerate(moves)]
    for copy in copies:
        copy.start()
    for copy in copies:
        copy.wait()


def shards(q, k, v, x, ld, sw, sr, doc, do, cm):
    tokens = q.shape[0]
    assert k.shape[1] == 2 * HEAD_CHANNELS
    wide = q.shape[1] // 2
    heads = ld.shape[1]
    states = sw.shape[1]
    chunk_cols = x.shape[1] // CHUNKS
    span = 3 * tokens
    square = (tokens, HEAD_CHANNELS)
    vmem = pltpu.VMEM
    hbm = pl.BlockSpec(memory_space=pltpu.HBM)
    onchip = pl.BlockSpec(memory_space=pltpu.VMEM)
    shape = jax.ShapeDtypeStruct
    operands = [
        pltpu.with_memory_space_constraint(a, pltpu.HBM) for a in (q, k, v, x, ld.T, sw, sr, doc.reshape(1, tokens), do, cm)
    ]
    parts = pl.pallas_call(
        step_kernel,
        out_shape=(shape((2, tokens, wide), BF16), shape((2,) + x.shape, BF16), shape((2, 2) + square, BF16)),
        in_specs=[hbm] * 10,
        out_specs=[onchip] * 3,
        scratch_shapes=[
            vmem((2, tokens, wide), BF16),
            vmem((2, tokens, wide), BF16),
            vmem((2, CHUNKS, tokens, chunk_cols), BF16),
            vmem((heads, tokens), F32),
            vmem((2, tokens, states), BF16),
            vmem((2, states, tokens), F32),
            vmem((5, 1, tokens), jnp.int32),
            vmem((2, 2) + square, BF16),
            vmem((4, 2) + square, BF16),
            vmem((2, tokens, 2 * heads), BF16),
            vmem((2, CHUNKS, heads // CHUNKS, tokens), F32),
            vmem((2, CHUNKS, tokens, chunk_cols), F32),
            vmem((CHUNKS, heads // CHUNKS, tokens), F32),
            vmem((2, CHUNKS, states, chunk_cols), BF16),
            vmem((CHUNKS, states, chunk_cols), BF16),
            vmem((CHUNKS, states, chunk_cols), BF16),
            vmem((CHUNKS, states, chunk_cols), BF16),
            vmem((CHUNKS, states, chunk_cols), BF16),
            vmem((CHUNKS, 1, chunk_cols), F32),
            vmem((CHUNKS, 1, chunk_cols), F32),
            vmem((2, CHUNKS, tokens, chunk_cols), F32),
            vmem((wide // HEAD_CHANNELS // 2, span, 2 * tokens), BF16),
            vmem((wide // HEAD_CHANNELS // 2, span, 2 * tokens), BF16),
            vmem((span, tokens), F32),
            vmem((2, tokens, wide), BF16),
            vmem((tokens, wide), BF16),
            vmem((2, 2) + square, BF16),
            vmem((4, 2) + square, F32),
            vmem((2, 2) + square, BF16),
            vmem((2,) + square, BF16),
            vmem((2,) + square, BF16),
            vmem((2, tokens, tokens), F32),
            pltpu.SemaphoreType.DMA((7,)),
            pltpu.SemaphoreType.DMA((17,)),
            pltpu.SemaphoreType.DMA((14 + 3 * CHUNKS,)),
            pltpu.SemaphoreType.REGULAR,
        ],
        compiler_params=pltpu.CompilerParams(collective_id=0, has_side_effects=True, vmem_limit_bytes=40 << 20),
        name="step",
    )(*operands)
    return pl.pallas_call(
        store_kernel,
        out_shape=(
            shape(q.shape, BF16), shape(x.shape, BF16), shape(k.shape, BF16), shape(v.shape, BF16), shape(x.shape, BF16),
        ),
        in_specs=[onchip] * 3,
        out_specs=[hbm] * 5,
        scratch_shapes=[pltpu.SemaphoreType.DMA((8,))],
        compiler_params=pltpu.CompilerParams(vmem_limit_bytes=8 << 20),
        name="store",
    )(*parts)


def solution(mesh):
    both = P("ctx", "tp")
    return jax.shard_map(
        shards,
        mesh=mesh,
        in_specs=(both, both, both, both, both, P("ctx", None), P("ctx", None), P("ctx"), both, both),
        out_specs=(both,) * 5,
        check_vma=False,
    )
```

```python
import math

import jax
import jax.numpy as jnp
from jax import lax
from jax.experimental import pallas as pl
from jax.experimental.pallas import tpu as pltpu
from jax.sharding import PartitionSpec as P

HEAD_CHANNELS = 128
CHUNKS = 4
DOUBLED = 256
ROUND = 16
MESH = pl.DeviceIdType.MESH
F32 = jnp.float32
BF16 = jnp.bfloat16


def dot(a, b, contract=((1,), (0,))):
    return lax.dot_general(a, b, (contract, ((), ())), preferred_element_type=F32)


def bf16_parts(values, count):
    parts = []
    for _ in range(count):
        parts.append(values.astype(BF16))
        values = values - parts[-1].astype(F32)
    return jnp.concatenate(parts, axis=0)


def step_kernel(
    q_in, k_in, v_in, x_in, ld_in, sw_in, sr_in, doc_in, do_in, cm_in,
    ao, mix, gkv,
    qw, dow, xc, ldb, srw, srwt, docs, kvo, kvw, scale, wrow, sc, lt, st, mbuf, cz, zbuf, lbuf, gain, gmate,
    local, pt, dst, bias, aob, aom, gs, gacc, gr, gsm, grm, gmask, lsem, ssem, rsem, ready,
):
    tokens = qw.shape[1]
    wide = qw.shape[2]
    heads = ld_in.shape[0]
    per_group = wide // HEAD_CHANNELS
    chunk_cols = x_in.shape[1] // CHUNKS
    chunk_heads = heads // CHUNKS
    half = chunk_cols // chunk_heads
    inv_root = 1.0 / math.sqrt(HEAD_CHANNELS)
    square = (tokens, tokens)

    count = lax.axis_size("ctx")
    me = lax.axis_index("ctx")
    row = lax.axis_index("tp")
    side = lax.rem(me, 2)
    other = 1 - side
    own = 2 + side
    mate = me + 1 - 2 * side
    outer = me - 1 + 2 * side
    before = [me - side - 2, me - side - 1]
    after = [me - side + 2, me - side + 3]
    has_before = me >= 2
    has_after = me < count - 2
    is_first = side == 0
    at_front = has_before & (lax.rem(me, ROUND) < 2)
    at_back = has_after & (lax.rem(me, ROUND) >= ROUND - 2)
    has_outer = (is_first & has_before) | (jnp.logical_not(is_first) & has_after)

    sems = {}

    def sem(kind, name, width=1):
        ref, used = {"local": (lsem, 0), "send": (ssem, 1), "recv": (rsem, 2)}[kind]
        if (kind, name) not in sems:
            sems[kind, name] = sems.get(used, 0)
            sems[used] = sems.get(used, 0) + width
        return ref, sems[kind, name]

    def drain(kind, name, ref, at=0):
        array, first = sem(kind, name)
        pltpu.make_async_copy(ref, ref, array.at[first + at]).wait()

    def load(name, src, dst_ref):
        array, first = sem("local", name)
        pltpu.make_async_copy(src, dst_ref, array.at[first]).start()

    def send(name, src, dst_ref, target, at=0, width=1):
        out, out_first = sem("send", name)
        into, into_first = sem("recv", name, width)
        return pltpu.make_async_remote_copy(
            src_ref=src, dst_ref=dst_ref, send_sem=out.at[out_first], recv_sem=into.at[into_first + at],
            device_id=(target, row), device_id_type=MESH,
        )

    def each(copies, act, there):
        if there is None:
            for copy in copies:
                act(copy)
        else:
            @pl.when(there)
            def _():
                for copy in copies:
                    act(copy)

    def start(copies, there=None):
        each(copies, lambda copy: copy.start(), there)

    def drained(kind, waits, there=None):
        each(waits, lambda wait: drain(kind, *wait), there)

    def over(count, body):
        lax.fori_loop(0, count, lambda c, carry: (body(c), carry)[1], 0)

    def part(which, width):
        return pl.ds(pl.multiple_of(which * width, width), width)

    docs_mate = send("docs_mate", docs.at[own], docs.at[own], mate)
    docs_after = [send("docs_after", docs.at[own], docs.at[side], after[h]) for h in range(2)]
    docs_before = [send("docs_before", docs.at[2], docs.at[4], before[h]) for h in range(2)]
    kv_mate = send("kv_mate", kvo.at[other], kvw.at[own], mate)
    kv_after = [send("kv_after", kvo.at[h], kvw.at[side], after[h]) for h in range(2)]
    q_mate = send("q_mate", q_in.at[:, part(other, wide)], qw.at[side], mate)
    do_mate = send("q_mate", do_in.at[:, part(other, wide)], dow.at[side], mate)
    gain_send = send("gain", gain, gmate, mate)
    ao_mate = send("ao", aob.at[other], aom, mate)
    grads_mate = send("grads_mate", gsm, grm, mate)
    sem("recv", "mate", CHUNKS)
    sem("recv", "outer", CHUNKS)
    sem("recv", "relay", CHUNKS)

    def grads_before(h):
        return send("grads", gs.at[h], gr.at[side], before[0] + h)

    def mate_send(c):
        return send("mate", st.at[side, c], mbuf.at[c], mate, c)

    def outer_send(c):
        return send("outer", cz.at[c], zbuf.at[c], outer, c)

    def relay_send(c):
        return send("relay", zbuf.at[c], lbuf.at[c], mate, c)

    last = CHUNKS - 1
    halves = [pl.ds(0, chunk_cols - DOUBLED), pl.ds(chunk_cols - DOUBLED, DOUBLED)]
    low_send = send("low", cz.at[last, :, halves[0]], zbuf.at[last, :, halves[0]], outer)
    high_send = send("high", cz.at[last, :, halves[1]], zbuf.at[last, :, halves[1]], outer)
    far_send = send("far", cz.at[last, :, halves[1]], lbuf.at[last, :, halves[1]], outer - 1 + 2 * side)
    low_relay = send("low_relay", zbuf.at[last, :, halves[0]], lbuf.at[last, :, halves[0]], mate)

    barrier = pltpu.get_barrier_semaphore()

    def tell(semaphore, targets, there=None):
        each(
            targets,
            lambda target: pl.semaphore_signal(semaphore, inc=1, device_id=(target, row), device_id_type=MESH),
            there,
        )

    tell(barrier, [mate])
    tell(barrier, before, has_before)
    tell(barrier, after, has_after & jnp.logical_not(at_back))

    load("doc", doc_in, docs.at[own])
    for h in range(2):
        cols = pl.ds(h * HEAD_CHANNELS, HEAD_CHANNELS)
        load("kv", k_in.at[:, cols], kvo.at[h, 0])
        load("kv", v_in.at[:, cols], kvo.at[h, 1])
    load("ld", ld_in, ldb)
    load("states", sw_in, srw.at[0])
    load("states", sr_in, srw.at[1])
    for d, src in enumerate((x_in, cm_in)):
        for c in range(CHUNKS):
            load("x", src.at[:, pl.ds(c * chunk_cols, chunk_cols)], xc.at[d, c])
    load("own_kv", k_in.at[:, part(side, HEAD_CHANNELS)], kvw.at[own, 0])
    load("own_kv", v_in.at[:, part(side, HEAD_CHANNELS)], kvw.at[own, 1])
    load("q", q_in.at[:, part(side, wide)], qw.at[side])
    load("q", do_in.at[:, part(side, wide)], dow.at[side])

    @pl.when(jnp.logical_not(has_before))
    def _():
        for h in range(2):
            docs[h] = jnp.full(docs.shape[1:], -1, jnp.int32)
            kvw[h] = jnp.zeros(kvw.shape[1:], BF16)

    @pl.when(jnp.logical_not(has_after))
    def _():
        docs[4] = jnp.full(docs.shape[1:], -1, jnp.int32)
        gr[...] = jnp.zeros(gr.shape, BF16)

    @pl.when(jnp.logical_not(has_outer))
    def _():
        zbuf[...] = jnp.zeros(zbuf.shape, BF16)

    @pl.when(jnp.logical_not(is_first | has_before))
    def _():
        lbuf[last] = jnp.zeros(lbuf.shape[1:], BF16)

    def announce():
        greeted = (has_before & jnp.logical_not(at_front)).astype(jnp.int32) + has_after.astype(jnp.int32)
        pl.semaphore_wait(barrier, 1 + 2 * greeted)
        tell(ready, after, at_back)
        start([docs_mate])
        start(docs_after + kv_after, has_after)
        start(docs_before, has_before & is_first & jnp.logical_not(at_front))
        start([kv_mate, q_mate, do_mate])

    sends_early = lax.rem(me, ROUND) >= ROUND // 2
    drained("local", [("doc", docs.at[own]), ("kv", kvo)])

    @pl.when(sends_early)
    def _():
        announce()

    rows_i = lax.broadcasted_iota(jnp.int32, square, 0)
    cols_i = lax.broadcasted_iota(jnp.int32, square, 1)
    triu = (rows_i <= cols_i).astype(F32).astype(BF16)
    drained("local", [("ld", ldb)])
    sums = dot(bf16_parts(ldb[...], 3), triu)
    lam_t = (sums[2 * heads :] + sums[heads : 2 * heads]) + sums[:heads]
    for c in range(CHUNKS):
        lt[c] = lam_t[c * chunk_heads : (c + 1) * chunk_heads]
    exits = jnp.exp(lam_t[:, tokens - 1 : tokens] - lam_t)
    entries = jnp.exp(lam_t)
    for c in range(CHUNKS):
        wrow[0, c] = exits[c * chunk_heads : (c + 1) * chunk_heads]
        wrow[1, c] = entries[c * chunk_heads : (c + 1) * chunk_heads]

    doc_row = docs[own].astype(F32)
    doc_first = doc_row[:, 0:1]
    doc_last = doc_row[:, tokens - 1 : tokens]
    doc_rows = jnp.broadcast_to(doc_row, square)
    doc_cols = doc_rows.T
    drained("local", [("states", srw)])
    writes = srw[0]
    reads = srw[1]
    writes_in = jnp.where(doc_cols == doc_last, writes.astype(F32), 0.0)
    reads_in = jnp.where(doc_cols == doc_first, reads.astype(F32), 0.0)
    srw[0] = writes_in.astype(BF16)
    srw[1] = reads_in.astype(BF16)
    srwt[0] = writes_in.T
    srwt[1] = reads_in.T

    lane = lax.broadcasted_iota(jnp.int32, (1, 2 * half), 1)
    low_half = (lane < half).astype(F32).astype(BF16)
    high_half = (lane >= half).astype(F32).astype(BF16)

    def two_heads(tile):
        return jnp.concatenate([tile * low_half, tile * high_half], axis=0)

    def state(d, c):
        weights = wrow[d, c]
        for j in range(chunk_heads // 2):
            cols = slice(2 * j * half, (2 * j + 2) * half)
            left_side = [(srwt[d] * weights[h : h + 1]).astype(BF16) for h in (2 * j, 2 * j + 1)]
            st[d, c, :, cols] = dot(jnp.concatenate(left_side, axis=1), two_heads(xc[d, c, :, cols])).astype(BF16)

    drained("local", [("x", xc)])

    def first_state(c):
        state(side, c)
        start([mate_send(c)], sends_early)

    over(CHUNKS, first_state)

    @pl.when(jnp.logical_not(sends_early))
    def _():
        announce()
        over(CHUNKS, lambda c: mate_send(c).start())

    over(CHUNKS, lambda c: state(other, c))

    whole = (doc_first == doc_last).astype(F32)

    def gains(c):
        ends = wrow[1, c][:, tokens - 1 : tokens] * whole
        pairs = [
            jnp.where(lane < half, ends[h : h + 1], ends[h + 1 : h + 2]) for h in range(0, chunk_heads, 2)
        ]
        gain[c] = jnp.concatenate(pairs, axis=1)

    over(CHUNKS, gains)
    start([gain_send])

    def edge(early, late):
        ends = docs[early].astype(F32)[:, tokens - 1 : tokens]
        return (docs[late].astype(F32)[:, 0:1] == ends).astype(F32)

    drained("recv", [("docs_mate", docs.at[own])])
    joined = edge(2, 3)

    def combine(c):
        drain("recv", "mate", mbuf.at[c], c)
        cz[c] = (st[other, c].astype(F32) + (gain[c] * joined) * mbuf[c].astype(F32)).astype(BF16)
        start([outer_send(c)], has_outer & (is_first | (c < last)))

    @pl.when(at_front & is_first)
    def _():
        pl.semaphore_wait(ready, 2)
        start(docs_before)

    over(CHUNKS, combine)
    start([low_send, far_send, high_send], has_outer & jnp.logical_not(is_first))

    scale[0] = bf16_parts(exits, 2).T
    scale[1] = bf16_parts(entries, 2).T
    spread_at = lax.broadcasted_iota(jnp.int32, (2 * heads, chunk_cols), 0)
    spread_head = lax.broadcasted_iota(jnp.int32, (2 * heads, chunk_cols), 1) // half

    same = doc_rows == doc_cols
    gmask[0] = jnp.where(same & (rows_i >= cols_i), dot(reads, writes, ((1,), (1,))), 0.0)
    gmask[1] = jnp.where(same & (cols_i >= rows_i), dot(writes, reads, ((1,), (1,))), 0.0)

    def inside_block(c):
        head = spread_head + c * chunk_heads
        hot = ((spread_at == head) | (spread_at == head + heads)).astype(F32).astype(BF16)
        for d in range(2):
            sc[d, c] = dot(scale[d], hot)
        for j in range(chunk_heads // 2):
            fwd = []
            bwd = []
            for h in (2 * j, 2 * j + 1):
                lam_rows = jnp.broadcast_to(lt[c, h : h + 1, :], square)
                decay = jnp.exp(-jnp.abs(lam_rows.T - lam_rows))
                fwd.append((decay * gmask[0]).astype(BF16))
                bwd.append((decay * gmask[1]).astype(BF16))
            cols = slice(2 * j * half, (2 * j + 2) * half)
            for d, weights in ((0, fwd), (1, bwd)):
                local[d, c, :, cols] = dot(jnp.concatenate(weights, axis=1), two_heads(xc[d, c, :, cols]))

    over(CHUNKS, inside_block)

    @pl.when(at_front & jnp.logical_not(is_first))
    def _():
        pl.semaphore_wait(ready, 2)

    drained("local", [("own_kv", kvw.at[own]), ("q", qw)])
    drained("recv", [("q_mate", qw), ("kv_mate", kvw.at[own])])
    drained("recv", [("docs_after", docs.at[0:2]), ("kv_after", kvw.at[0:2])], has_before)
    gacc[...] = jnp.zeros(gacc.shape, F32)

    def attend(pos):
        rows = jnp.broadcast_to(docs[2 + pos].astype(F32), square)
        for n in range(3):
            keep = jnp.broadcast_to(docs[pos + n].astype(F32), square).T == rows
            if n == 2:
                keep = keep & (cols_i >= rows_i)
            bias[n * tokens : (n + 1) * tokens] = jnp.where(keep, 0.0, -1e30)

        def two_queries(pair):
            def pair_of(ref):
                return jnp.concatenate(
                    [ref[pos, :, pl.ds(pl.multiple_of((2 * pair + i) * HEAD_CHANNELS, HEAD_CHANNELS), HEAD_CHANNELS)] for i in range(2)],
                    axis=0,
                )

            keys = jnp.concatenate([kvw[pos + n, 0] for n in range(3)], axis=0)
            values = jnp.concatenate([kvw[pos + n, 1] for n in range(3)], axis=0)
            mask = jnp.concatenate([bias[...], bias[...]], axis=1)
            raw = dot(keys, pair_of(qw), ((1,), (1,))) + mask
            peak = jnp.max(raw, axis=0, keepdims=True)
            raised = jnp.exp((raw - peak) * inv_root)
            probs = (raised * (1.0 / jnp.sum(raised, axis=0, keepdims=True))).astype(BF16)
            pt[pair] = probs
            out_t = dot(values.T, probs)
            for i in range(2):
                cols = pl.ds(pl.multiple_of((2 * pair + i) * HEAD_CHANNELS, HEAD_CHANNELS), HEAD_CHANNELS)
                aob[pos, :, cols] = out_t[:, i * tokens : (i + 1) * tokens].T.astype(BF16)
            prob_grad = dot(values, pair_of(dow), ((1,), (1,)))
            single = probs.astype(F32)
            inner = jnp.sum(single * prob_grad, axis=0, keepdims=True)
            dst[pair] = (single * (prob_grad - inner) * inv_root).astype(BF16)

        over(per_group // 2, two_queries)
        for n, (probs_ref, rows_ref) in enumerate(((dst, qw), (pt, dow))):
            grad = dot(
                jnp.concatenate([probs_ref[pair] for pair in range(per_group // 2)], axis=1),
                jnp.concatenate(
                    [rows_ref[pos, :, i * HEAD_CHANNELS : (i + 1) * HEAD_CHANNELS] for i in range(per_group)], axis=0
                ),
            )
            for m in range(3):
                gacc[pos + m, n] += grad[m * tokens : (m + 1) * tokens]
            gs[pos, n] = gacc[pos, n].astype(BF16)
        start([grads_before(pos)], has_before)

    over(2, attend)
    start([ao_mate])
    for n in range(2):
        gsm[n] = gacc[2 + other, n].astype(BF16)
    start([grads_mate])
    ao[side] = aob[side]

    drained("recv", [("docs_before", docs.at[4])], has_after)
    in_before = edge(1, 2)
    in_after = edge(3, 4)
    outer_joined = jnp.where(is_first, in_before, in_after)
    mate_joined = jnp.where(is_first, in_after, in_before)

    def finish(d, c, rows, carried):
        mix[d, :, part(c, chunk_cols)] = (local[d, c] + sc[1 - d, c] * dot(rows, carried)).astype(BF16)

    rows = (srw[other].astype(F32) * outer_joined).astype(BF16)

    mate_rows = (srw[side].astype(F32) * joined).astype(BF16)

    def carry_from_mate(c):
        carried = mbuf[c].astype(F32) + (gmate[c] * mate_joined) * lbuf[c].astype(F32)
        finish(other, c, mate_rows, carried.astype(BF16))

    def from_mate(c):
        drain("recv", "relay", lbuf.at[c], c)
        carry_from_mate(c)

    def carries_from_mate():
        drained("recv", [("gain", gain)])
        over(last, from_mate)

        @pl.when(at_front & jnp.logical_not(is_first))
        def _():
            gradients()

        @pl.when(is_first)
        def _():
            drained("recv", [("relay", lbuf.at[last], last)])

        @pl.when(jnp.logical_not(is_first))
        def _():
            drained("recv", [("low_relay", lbuf.at[last, :, halves[0]])])
            drained("recv", [("far", lbuf.at[last, :, halves[1]])], has_before)

        carry_from_mate(last)

    def gradients():
        drained("recv", [("ao", aom), ("grads_mate", grm)])
        ao[other] = aom[...]
        drained("recv", [("grads", gr)], has_after)
        for n in range(2):
            gkv[side, n] = (gacc[own, n] + gr[side, n].astype(F32)).astype(BF16)
            gkv[other, n] = (grm[n].astype(F32) + gr[other, n].astype(F32)).astype(BF16)

    def from_outside(c):
        drained("recv", [("outer", zbuf.at[c], c)], has_outer)
        relay_send(c).start()
        finish(side, c, rows, zbuf[c])

    over(last, from_outside)

    @pl.when(is_first)
    def _():
        drained("recv", [("low", zbuf.at[last, :, halves[0]])], has_outer)
        low_relay.start()

        @pl.when(at_front)
        def _():
            carries_from_mate()
            gradients()

        drained("recv", [("high", zbuf.at[last, :, halves[1]])], has_outer)

    @pl.when(jnp.logical_not(is_first))
    def _():
        drained("recv", [("outer", zbuf.at[last], last)], has_outer)
        relay_send(last).start()

    finish(side, last, rows, zbuf[last])
    sent = [("docs_mate", docs.at[own]), ("kv_mate", kvo.at[0]), ("q_mate", qw), ("gain", gain), ("mate", mbuf)]
    drained("send", sent)
    drained("send", [("docs_after", docs.at[0:2]), ("kv_after", kvo)], has_after)
    drained("send", [("docs_before", docs.at[0:2])], has_before & is_first)
    drained("send", [("outer", cz)], has_outer & is_first)
    low_part, high_part = (cz.at[last, :, cols] for cols in halves)
    drained(
        "send",
        [("outer", cz.at[0:last]), ("low", low_part), ("high", high_part), ("far", high_part)],
        has_outer & jnp.logical_not(is_first),
    )

    @pl.when(jnp.logical_not(at_front & is_first))
    def _():
        carries_from_mate()

    @pl.when(jnp.logical_not(at_front))
    def _():
        gradients()

    drained("send", [("ao", aom), ("grads_mate", gsm)])
    drained("send", [("grads", gs)], has_before)
    drained("send", [("relay", zbuf.at[0:last]), ("low_relay", low_part)], is_first)
    drained("send", [("relay", zbuf)], jnp.logical_not(is_first))


def store_kernel(ao, mix, gkv, ao_out, mo_out, gk_out, gv_out, gx_out, sem):
    moves = [(mix.at[0], mo_out), (mix.at[1], gx_out)]
    for h in range(2):
        wide = ao.shape[2]
        moves.append((ao.at[h], ao_out.at[:, pl.ds(h * wide, wide)]))
        for n, out in enumerate((gk_out, gv_out)):
            moves.append((gkv.at[h, n], out.at[:, pl.ds(h * HEAD_CHANNELS, HEAD_CHANNELS)]))
    copies = [pltpu.make_async_copy(src, dst, sem.at[n]) for n, (src, dst) in enumerate(moves)]
    for copy in copies:
        copy.start()
    for copy in copies:
        copy.wait()


def shards(q, k, v, x, ld, sw, sr, doc, do, cm):
    tokens = q.shape[0]
    assert k.shape[1] == 2 * HEAD_CHANNELS
    wide = q.shape[1] // 2
    heads = ld.shape[1]
    states = sw.shape[1]
    chunk_cols = x.shape[1] // CHUNKS
    span = 3 * tokens
    square = (tokens, HEAD_CHANNELS)
    vmem = pltpu.VMEM
    hbm = pl.BlockSpec(memory_space=pltpu.HBM)
    onchip = pl.BlockSpec(memory_space=pltpu.VMEM)
    shape = jax.ShapeDtypeStruct
    operands = [
        pltpu.with_memory_space_constraint(a, pltpu.HBM) for a in (q, k, v, x, ld.T, sw, sr, doc.reshape(1, tokens), do, cm)
    ]
    parts = pl.pallas_call(
        step_kernel,
        out_shape=(shape((2, tokens, wide), BF16), shape((2,) + x.shape, BF16), shape((2, 2) + square, BF16)),
        in_specs=[hbm] * 10,
        out_specs=[onchip] * 3,
        scratch_shapes=[
            vmem((2, tokens, wide), BF16),
            vmem((2, tokens, wide), BF16),
            vmem((2, CHUNKS, tokens, chunk_cols), BF16),
            vmem((heads, tokens), F32),
            vmem((2, tokens, states), BF16),
            vmem((2, states, tokens), F32),
            vmem((5, 1, tokens), jnp.int32),
            vmem((2, 2) + square, BF16),
            vmem((4, 2) + square, BF16),
            vmem((2, tokens, 2 * heads), BF16),
            vmem((2, CHUNKS, heads // CHUNKS, tokens), F32),
            vmem((2, CHUNKS, tokens, chunk_cols), F32),
            vmem((CHUNKS, heads // CHUNKS, tokens), F32),
            vmem((2, CHUNKS, states, chunk_cols), BF16),
            vmem((CHUNKS, states, chunk_cols), BF16),
            vmem((CHUNKS, states, chunk_cols), BF16),
            vmem((CHUNKS, states, chunk_cols), BF16),
            vmem((CHUNKS, states, chunk_cols), BF16),
            vmem((CHUNKS, 1, chunk_cols), F32),
            vmem((CHUNKS, 1, chunk_cols), F32),
            vmem((2, CHUNKS, tokens, chunk_cols), F32),
            vmem((wide // HEAD_CHANNELS // 2, span, 2 * tokens), BF16),
            vmem((wide // HEAD_CHANNELS // 2, span, 2 * tokens), BF16),
            vmem((span, tokens), F32),
            vmem((2, tokens, wide), BF16),
            vmem((tokens, wide), BF16),
            vmem((2, 2) + square, BF16),
            vmem((4, 2) + square, F32),
            vmem((2, 2) + square, BF16),
            vmem((2,) + square, BF16),
            vmem((2,) + square, BF16),
            vmem((2, tokens, tokens), F32),
            pltpu.SemaphoreType.DMA((7,)),
            pltpu.SemaphoreType.DMA((17,)),
            pltpu.SemaphoreType.DMA((14 + 3 * CHUNKS,)),
            pltpu.SemaphoreType.REGULAR,
        ],
        compiler_params=pltpu.CompilerParams(collective_id=0, has_side_effects=True, vmem_limit_bytes=40 << 20),
        name="step",
    )(*operands)
    return pl.pallas_call(
        store_kernel,
        out_shape=(
            shape(q.shape, BF16), shape(x.shape, BF16), shape(k.shape, BF16), shape(v.shape, BF16), shape(x.shape, BF16),
        ),
        in_specs=[onchip] * 3,
        out_specs=[hbm] * 5,
        scratch_shapes=[pltpu.SemaphoreType.DMA((8,))],
        compiler_params=pltpu.CompilerParams(vmem_limit_bytes=8 << 20),
        name="store",
    )(*parts)


def solution(mesh):
    both = P("ctx", "tp")
    return jax.shard_map(
        shards,
        mesh=mesh,
        in_specs=(both, both, both, both, both, P("ctx", None), P("ctx", None), P("ctx"), both, both),
        out_specs=(both,) * 5,
        check_vma=False,
    )
```
